512 devices in a mesh: section: 4 (over y_lo), rows: 128 (over x, z, y_hi, core).
Axes of the slice: x: 4, y: 8 (y_hi: 2, y_lo: 4; y = y_hi * 4 + y_lo), z: 8, core: 2. Of those that a mesh axis runs over, the one named last changes fastest.
Arguments:
- latents: bfloat16 [4, 8, 4, 640], P(None, None, None, 'rows'), may hold values from -20 to 20
- w_in: bfloat16 [3, 4, 512], replicated, may hold values from -1.75 to 1.75
- w_time: bfloat16 [3, 512, 512], replicated, may hold values from -0.15625 to 0.15625
- w_first: bfloat16 [3, 3, 512, 512], P(None, None, None, 'section'), may hold values from -0.09375 to 0.09375
- w_second: bfloat16 [3, 3, 512, 512], P(None, None, None, 'section'), may hold values from -0.09375 to 0.09375
Outputs:
- decoded: bfloat16 [128, 4, 160, 512], P('rows', None, None, 'section')
The draws below stay inside these ranges and needn't reach their ends.
All inputs are finite; a program needn't handle non-finite values.
Results may differ from the reference program's by a relative error of at most 0.0064.
Values may be sent and summed in bfloat16 or wider, within the bound.
No kernel may reach another device: no remote copies, remote signals or barrier semaphores. Data moves between devices by JAX's collectives and lax.ppermute only.
A program may use at most 64 MiB of HBM per device.

```python
import math
import jax
import jax.numpy as jnp
from jax import lax

CH = 512
LATC = 4
GROUPS = 32
HS = 4
W = 160
CLIPS = 4
LF = 8
UPS = 4
FR = 32
FRAMES = 128
POS = 640


def draw_latents(key, part):
    key_base, key_rows, key_cols = jax.random.split(key, 3)
    base = jax.random.truncated_normal(key_base, -4.0, 4.0, (CLIPS, LF, LATC, HS, W), jnp.float32)
    row_scale = jnp.exp(jax.random.uniform(key_rows, (CLIPS, LF, 1, HS, 1), jnp.float32, math.log(0.3), math.log(3.0)))
    col_scale = jnp.exp(jax.random.uniform(key_cols, (1, 1, 1, 1, W), jnp.float32, math.log(0.5), math.log(1.6)))
    return (base * row_scale * col_scale).reshape(CLIPS, LF, LATC, HS * W).astype(jnp.bfloat16)


def block_scale(rng, extent, pieces, low, high):
    loudness = 1.0
    for dim, blocks in pieces:
        heights = jax.random.uniform(jax.random.fold_in(jax.random.fold_in(rng, 6), dim), (blocks,), jnp.float32, low / len(pieces), high / len(pieces))
        loudness = loudness * jnp.repeat(jnp.exp(heights), extent[dim] // blocks).reshape((-1,) + (1,) * (len(extent) - 1 - dim))
    return loudness


def scatter_about(rng, shape, spread, most, cuts=(), kind=jnp.bfloat16):
    entries = jax.random.normal(rng, shape, jnp.float32) * spread
    if len(cuts) > 0:
        entries = block_scale(rng, shape, cuts, -0.22, 0.18) * entries
    return jnp.clip(entries, min=-most, max=most).astype(kind)


def setup_inputs(seed: int = 0) -> dict:
    seeds = jax.random.split(jax.random.key(seed), 6)
    return {
        "latents": draw_latents(jax.random.fold_in(seeds[5], 71), 0),
        "w_in": scatter_about(seeds[1], (3, LATC, CH), (3 * LATC) ** -0.5, 1.75),
        "w_time": scatter_about(seeds[2], (3, CH, CH), (3 * CH) ** -0.5, 0.15625),
        "w_first": scatter_about(seeds[3], (3, 3, CH, CH), (9 * CH) ** -0.5, 0.09375, ((3, 4),)),
        "w_second": scatter_about(seeds[4], (3, 3, CH, CH), (9 * CH) ** -0.5, 0.09375, ((3, 4),)),
    }


def causal_taps(length, offset):
    return jnp.maximum(jnp.arange(length) - 2 + offset, 0)

def group_norm(values):
    frames, height, width, channels = values.shape
    grouped = values.reshape(frames, height, width, GROUPS, channels // GROUPS)
    mean = lax.optimization_barrier(jnp.mean(grouped, axis=(1, 2, 4), keepdims=True))
    centered = grouped - mean
    variance = lax.optimization_barrier(jnp.mean(centered * centered, axis=(1, 2, 4), keepdims=True))
    return (centered * lax.rsqrt(variance + 1e-06)).reshape(values.shape)

def conv_grid(image, weight):
    return lax.conv_general_dilated(image.astype(jnp.float32), weight.astype(jnp.float32), (1, 1), 'SAME', dimension_numbers=('NHWC', 'HWIO', 'NHWC'), precision=lax.Precision.HIGHEST)

def reference(latents, w_in, w_time, w_first, w_second):
    summed = jnp.zeros((CLIPS, LF, POS, CH), jnp.float32)
    for offset in range(3):
        picked = latents[:, causal_taps(LF, offset)]
        summed = summed + jnp.einsum('clqp,qh->clph', picked.astype(jnp.float32), w_in[offset].astype(jnp.float32), precision=lax.Precision.HIGHEST)
    lat_feats = summed.astype(jnp.bfloat16)
    upsampled = jnp.repeat(lat_feats, UPS, axis=1)
    activated = jax.nn.silu(upsampled.astype(jnp.float32)).astype(jnp.bfloat16)
    mixed = upsampled.astype(jnp.float32)
    for offset in range(3):
        shifted = activated[:, causal_taps(FR, offset)]
        mixed = mixed + jnp.einsum('cfph,hg->cfpg', shifted.astype(jnp.float32), w_time[offset].astype(jnp.float32), precision=lax.Precision.HIGHEST)
    temporal = mixed.astype(jnp.bfloat16).reshape(FRAMES, HS, W, CH)
    first_in = jax.nn.silu(group_norm(temporal.astype(jnp.float32))).astype(jnp.bfloat16)
    inner = conv_grid(first_in, w_first).astype(jnp.bfloat16)
    second_in = jax.nn.silu(group_norm(inner.astype(jnp.float32))).astype(jnp.bfloat16)
    return (temporal.astype(jnp.float32) + conv_grid(second_in, w_second)).astype(jnp.bfloat16)
```

```python
import jax
import jax.numpy as jnp
from jax import lax
from jax.experimental import pallas as pl
from jax.experimental.pallas import tpu as pltpu
from jax.sharding import PartitionSpec as P

CH = 512
LATC = 4
HS = 4
W = 160
CELLS = HS * W
CLIPS = 4
LF = 8
UPS = 4
FRAMES = 128
GROUP = 16
LOCAL = 5
WINDOW = 4
MSG = LOCAL * WINDOW * LATC
STEP = 128

F32 = jnp.float32
BF16 = jnp.bfloat16


def dot(a, b):
    return jnp.dot(a, b, preferred_element_type=F32)


def iota(shape, dim):
    return lax.broadcasted_iota(jnp.int32, shape, dim)


def onehot(cond):
    return jnp.where(cond, 1.0, 0.0).astype(BF16)


def silu(t):
    return 0.5 * t * (1.0 + jnp.tanh(0.5 * t))


def pack_kernel(lat_ref, out_ref):
    lane = iota((LOCAL, MSG), 1)
    cell = iota((LOCAL, MSG), 0)
    spread = jnp.zeros((CLIPS * LF, MSG), F32)
    for ch in range(LATC):
        place = onehot((lane // 16 == cell) & (lane % LATC == ch))
        spread = spread + dot(lat_ref[:, ch, :], place)
    spread = spread.astype(BF16)
    frame = iota((FRAMES, CLIPS * LF), 0)
    row = iota((FRAMES, CLIPS * LF), 1)
    window_of = (iota((FRAMES, MSG), 1) // LATC) % WINDOW
    total = jnp.zeros((FRAMES, MSG), F32)
    for j in range(WINDOW):
        latent = jnp.maximum((frame % 32) // UPS - 3 + j, 0)
        pick = onehot(row == (frame // 32) * LF + latent)
        total = jnp.where(window_of == j, dot(pick, spread), total)
    out_ref[...] = total.astype(BF16)


def loop(body, rows=CELLS, step=STEP):
    def wrapped(i, carry):
        return body(pl.ds(pl.multiple_of(i * step, step), step), carry)
    return wrapped, rows // step


def group_total(sums):
    lane = iota(sums.shape, 1)
    width = sums.shape[1]
    for d in (1, 2, 4, 8):
        up = pltpu.roll(sums, d, 1)
        down = pltpu.roll(sums, width - d, 1)
        sums = sums + jnp.where((lane & d) != 0, up, down)
    return sums


def norm_silu(src_ref, dst_ref, width):
    count = float(CELLS * GROUP)

    def add(rows, carry):
        return carry + jnp.sum(src_ref[rows, :].astype(F32).reshape(STEP // 8, 8, width), axis=0)

    def total(fn):
        body, n = loop(fn)
        part = lax.fori_loop(0, n, body, jnp.zeros((8, width), F32))
        part = jnp.sum(part, axis=0, keepdims=True)
        return group_total(jnp.broadcast_to(part, (8, width)))[:1] / count

    mean = total(add)

    def add_sq(rows, carry):
        t = src_ref[rows, :].astype(F32) - mean
        return carry + jnp.sum((t * t).reshape(STEP // 8, 8, width), axis=0)

    scale = lax.rsqrt(total(add_sq) + 1e-06)

    def write(rows, carry):
        t = (src_ref[rows, :].astype(F32) - mean) * scale
        dst_ref[rows, :] = silu(t).astype(BF16)
        return carry

    body, n = loop(write)
    lax.fori_loop(0, n, body, 0)


def conv(h_ref, w_ref, acc_ref):
    for n, dy in enumerate((1, 0, 2)):
        w = jnp.concatenate([w_ref[dy, dx] for dx in range(3)], axis=1)
        if dy == 1:
            acc_ref[...] = dot(h_ref[...], w)
        elif dy == 0:
            acc_ref[W:, :] += dot(h_ref[: CELLS - W, :], w)
        else:
            acc_ref[: CELLS - W, :] += dot(h_ref[W:, :], w)


def gathered(acc_ref, i):
    rows = slice(i * W, (i + 1) * W)
    col = iota((W, 128), 0)
    left = jnp.where(col == 0, 0.0, pltpu.roll(acc_ref[rows, 0:128], 1, 0))
    right = jnp.where(col == W - 1, 0.0, pltpu.roll(acc_ref[rows, 256:384], W - 1, 0))
    return left + acc_ref[rows, 128:256] + right


def first_kernel(sub_ref, recv_ref, w_in_ref, w_time_ref, w_first_ref, x_ref, h2_ref,
                 u_ref, v_ref, h_ref, acc_ref, h1_ref):
    src = iota((CELLS, FRAMES), 1)
    at = iota((CELLS, FRAMES), 0)
    spread = dot(onehot((at >= src * LOCAL) & (at < src * LOCAL + LOCAL)), recv_ref[...])
    lane = iota((CELLS, MSG), 1)
    own = iota((CELLS, MSG), 0) % LOCAL == lane // 16
    spread = jnp.where(own, spread, 0.0).astype(BF16)
    slot = iota((MSG, 16), 0) % 16
    col = iota((MSG, 16), 1)
    for s in range(2):
        picked = dot(spread, onehot(slot == col + s * LATC)).astype(BF16)
        u = dot(picked, w_in_ref[...]).astype(BF16)
        if s == 1:
            u_ref[...] = u
        v_ref[s] = silu(u.astype(F32)).astype(BF16)
    sub = sub_ref[0]
    total = u_ref[...].astype(F32)
    for k in range(3):
        which = (sub >= 2 - k).astype(jnp.int32)
        total = total + dot(v_ref[which], w_time_ref[k])
    x_ref[...] = total.astype(BF16)
    norm_silu(x_ref, h_ref, CH)
    conv(h_ref, w_first_ref, acc_ref)
    for i in range(HS):
        h1_ref[i * W : (i + 1) * W, :] = gathered(acc_ref, i).astype(BF16)
    norm_silu(h1_ref, h2_ref, 128)


def second_kernel(section_ref, x_ref, h_ref, w_ref, out_ref, acc_ref):
    conv(h_ref, w_ref, acc_ref)
    lanes = pl.ds(pl.multiple_of(section_ref[0] * 128, 128), 128)
    for i in range(HS):
        residual = x_ref[i * W : (i + 1) * W, lanes].astype(F32)
        out_ref[i] = (residual + gathered(acc_ref, i)).astype(BF16)


VM = pl.BlockSpec(memory_space=pltpu.VMEM)
SM = pl.BlockSpec(memory_space=pltpu.SMEM)


def per_device(latents, w_in, w_time, w_first, w_second):
    packed = pl.pallas_call(
        pack_kernel,
        out_shape=jax.ShapeDtypeStruct((FRAMES, MSG), BF16),
        in_specs=[VM],
        out_specs=VM,
    )(latents.reshape(CLIPS * LF, LATC, LOCAL))
    recv = lax.all_to_all(packed, "rows", split_axis=0, concat_axis=0, tiled=True)
    sub = (lax.axis_index("rows") % UPS).astype(jnp.int32).reshape(1)
    section = lax.axis_index("section").astype(jnp.int32).reshape(1)
    taps = jnp.pad(w_in.reshape(3 * LATC, CH), ((0, 4), (0, 0)))
    x, h2 = pl.pallas_call(
        first_kernel,
        out_shape=[
            jax.ShapeDtypeStruct((CELLS, CH), BF16),
            jax.ShapeDtypeStruct((CELLS, 128), BF16),
        ],
        in_specs=[SM, VM, VM, VM, VM],
        out_specs=[VM, VM],
        scratch_shapes=[
            pltpu.VMEM((CELLS, CH), BF16),
            pltpu.VMEM((2, CELLS, CH), BF16),
            pltpu.VMEM((CELLS, CH), BF16),
            pltpu.VMEM((CELLS, 384), F32),
            pltpu.VMEM((CELLS, 128), BF16),
        ],
    )(sub, recv, taps, w_time, w_first)
    h2_all = lax.all_gather(h2, "section", axis=1, tiled=True)
    out = pl.pallas_call(
        second_kernel,
        out_shape=jax.ShapeDtypeStruct((HS, W, 128), BF16),
        in_specs=[SM, VM, VM, VM],
        out_specs=VM,
        scratch_shapes=[pltpu.VMEM((CELLS, 384), F32)],
    )(section, x, h2_all, w_second)
    return out.reshape(1, HS, W, 128)


def solution(mesh):
    in_specs = (
        P(None, None, None, "rows"),
        P(),
        P(),
        P(None, None, None, "section"),
        P(None, None, None, "section"),
    )
    out_specs = P("rows", None, None, "section")
    return jax.shard_map(
        per_device, mesh=mesh, in_specs=in_specs, out_specs=out_specs, check_vma=False
    )
```

```python
import jax
import jax.numpy as jnp
from jax import lax
from jax.experimental import pallas as pl
from jax.experimental.pallas import tpu as pltpu
from jax.sharding import PartitionSpec as P


CH = 512
LATC = 4
HS = 4
W = 160
CELLS = HS * W
CLIPS = 4
LF = 8
UPS = 4
FRAMES = 128
GROUP = 16
LOCAL = 5
WINDOW = 4
MSG = LOCAL * WINDOW * LATC
STEP = 128

F32 = jnp.float32
BF16 = jnp.bfloat16


def dot(a, b):
    return jnp.dot(a, b, preferred_element_type=F32)


def iota(shape, dim):
    return lax.broadcasted_iota(jnp.int32, shape, dim)


def onehot(cond):
    return jnp.where(cond, 1.0, 0.0).astype(BF16)


def silu(t):
    return 0.5 * t * (1.0 + jnp.tanh(0.5 * t))


def pack_kernel(lat_ref, out_ref, flat_ref):
    for n in range(CLIPS * LOCAL):
        flat_ref[n * LATC : (n + 1) * LATC, :] = lat_ref[n].astype(F32)
    flat = flat_ref[...].astype(BF16)
    frame = iota((FRAMES, LF), 0)
    latent = iota((FRAMES, LF), 1)
    same_clip = iota((FRAMES, MSG), 0) // 32 == iota((FRAMES, MSG), 1) // (LOCAL * LATC)
    src = iota((MSG, MSG), 0) % (LOCAL * LATC)
    lane = iota((MSG, MSG), 1)
    home = (src // LATC == lane // 16) & (src % LATC == lane % LATC)
    total = jnp.zeros((FRAMES, MSG), F32)
    for j in range(WINDOW):
        pick = onehot(latent == jnp.maximum((frame % 32) // UPS - 3 + j, 0))
        taken = lax.dot_general(pick, flat, (((1,), (1,)), ((), ())), preferred_element_type=F32)
        taken = jnp.where(same_clip, taken, 0.0).astype(BF16)
        total = total + dot(taken, onehot(home & ((lane // LATC) % WINDOW == j)))
    out_ref[:, 0, :] = total.astype(BF16)


def loop(body, rows=CELLS, step=STEP):
    def wrapped(i, carry):
        return body(pl.ds(pl.multiple_of(i * step, step), step), carry)

    return wrapped, rows // step


def group_total(sums):
    lane = iota(sums.shape, 1)
    width = sums.shape[1]
    for d in (1, 2, 4, 8):
        up = pltpu.roll(sums, d, 1)
        down = pltpu.roll(sums, width - d, 1)
        sums = sums + jnp.where((lane & d) != 0, up, down)
    return sums


def norm_silu(src_ref, dst_ref, width):
    count = float(CELLS * GROUP)

    def add(rows, carry):
        return carry + jnp.sum(src_ref[rows, :].astype(F32).reshape(STEP // 8, 8, width), axis=0)

    def total(fn):
        body, n = loop(fn)
        part = lax.fori_loop(0, n, body, jnp.zeros((8, width), F32))
        part = jnp.sum(part, axis=0, keepdims=True)
        return group_total(jnp.broadcast_to(part, (8, width)))[:1] / count

    mean = total(add)

    def add_sq(rows, carry):
        t = src_ref[rows, :].astype(F32) - mean
        return carry + jnp.sum((t * t).reshape(STEP // 8, 8, width), axis=0)

    scale = lax.rsqrt(total(add_sq) + 1e-06)

    def write(rows, carry):
        t = (src_ref[rows, :].astype(F32) - mean) * scale
        dst_ref[rows, :] = silu(t).astype(BF16)
        return carry

    body, n = loop(write)
    lax.fori_loop(0, n, body, 0)


def conv(h_ref, parts, acc_ref):
    for dy in (1, 0, 2):
        src = slice(W, CELLS) if dy == 2 else slice(0, CELLS - W) if dy == 0 else slice(0, CELLS)
        dst = slice(W, CELLS) if dy == 0 else slice(0, CELLS - W) if dy == 2 else slice(0, CELLS)
        total = None
        for lanes, weights in parts:
            w = jnp.concatenate([ref[dy, dx] for ref in weights for dx in range(3)], axis=1)
            term = dot(h_ref[src, lanes], w)
            total = term if total is None else total + term
        if dy == 1:
            acc_ref[...] = total
        else:
            acc_ref[dst, :] += total


def gathered(acc_ref, i, base=0):
    rows = slice(i * W, (i + 1) * W)
    col = iota((W, 128), 0)
    left = jnp.where(col == 0, 0.0, pltpu.roll(acc_ref[rows, base : base + 128], 1, 0))
    right = jnp.where(col == W - 1, 0.0, pltpu.roll(acc_ref[rows, base + 256 : base + 384], W - 1, 0))
    return left + acc_ref[rows, base + 128 : base + 256] + right


def inner_quarters(h_ref, parts, acc_ref, h1_ref, h2_ref, count):
    conv(h_ref, parts, acc_ref)
    for n in range(count):
        for i in range(HS):
            h1_ref[i * W : (i + 1) * W, n * 128 : (n + 1) * 128] = gathered(acc_ref, i, n * 384).astype(BF16)
    norm_silu(h1_ref, h2_ref, count * 128)


def halves(core):
    mine = pl.ds(pl.multiple_of(core * 256, 256), 256)
    other = pl.ds(pl.multiple_of(256 - core * 256, 256), 256)
    return mine, other


def first_kernel(at_ref, recv_ref, w_in_ref, w_time_ref, own_ref, left_ref, right_ref, left_swap_ref, right_swap_ref,
                 x_ref, h_ref, mid_ref, side_ref, u_ref, v_ref, acc_ref, h1_ref, wide_ref, h1_wide_ref):
    src = iota((CELLS, FRAMES), 1)
    at = iota((CELLS, FRAMES), 0)
    spread = dot(onehot((at >= src * LOCAL) & (at < src * LOCAL + LOCAL)), recv_ref[:, 0, :])
    lane = iota((CELLS, MSG), 1)
    own = iota((CELLS, MSG), 0) % LOCAL == lane // 16
    spread = jnp.where(own, spread, 0.0).astype(BF16)
    slot = iota((MSG, 16), 0) % 16
    col = iota((MSG, 16), 1)
    for s in range(2):
        picked = dot(spread, onehot(slot == col + s * LATC)).astype(BF16)
        u = dot(picked, w_in_ref[...]).astype(BF16)
        if s == 1:
            u_ref[...] = u
        v_ref[s] = silu(u.astype(F32)).astype(BF16)
    sub = at_ref[0] % UPS
    total = u_ref[...].astype(F32)
    for k in range(3):
        which = (sub >= 2 - k).astype(jnp.int32)
        total = total + dot(v_ref[which], w_time_ref[k])
    x_ref[...] = total.astype(BF16)
    norm_silu(x_ref, h_ref, CH)
    mine, other = halves(at_ref[0] % 2)
    inner_quarters(h_ref, [(slice(0, CH), [own_ref])], acc_ref, h1_ref, mid_ref, 1)
    inner_quarters(h_ref, [(mine, [left_ref, right_ref]), (other, [left_swap_ref, right_swap_ref])],
                   wide_ref, h1_wide_ref, side_ref, 2)


def second_kernel(at_ref, x_ref, h_ref, mid_ref, side_ref, far_ref, far_swap_ref, w_ref, out_ref,
                  acc_ref, h1_ref, h2_ref, all_ref):
    mine, other = halves(at_ref[0] % 2)
    inner_quarters(h_ref, [(mine, [far_ref]), (other, [far_swap_ref])], acc_ref, h1_ref, h2_ref, 1)

    def lanes(shift):
        return pl.ds(pl.multiple_of(((at_ref[1] + shift) % 4) * 128, 128), 128)

    all_ref[:, lanes(0)] = mid_ref[...]
    all_ref[:, lanes(3)] = side_ref[:, :128]
    all_ref[:, lanes(1)] = side_ref[:, 128:]
    all_ref[:, lanes(2)] = h2_ref[...]
    conv(all_ref, [(slice(0, CH), [w_ref])], acc_ref)
    for i in range(HS):
        residual = x_ref[i * W : (i + 1) * W, lanes(0)].astype(F32)
        out_ref[i] = (residual + gathered(acc_ref, i)).astype(BF16)


VM = pl.BlockSpec(memory_space=pltpu.VMEM)
SM = pl.BlockSpec(memory_space=pltpu.SMEM)


def along_y(shift):
    pairs = []
    for row in range(FRAMES):
        for section in range(4):
            y = (4 * (row // 2 % 2) + section + shift) % 8
            there = row // 4 * 4 + y // 4 * 2 + row % 2
            pairs.append((section * FRAMES + row, y % 4 * FRAMES + there))
    return pairs


def move_y(value, shift):
    return lax.ppermute(value, ("section", "rows"), along_y(shift))


def swap(value):
    return lax.ppermute(value, "rows", [(row, row ^ 1) for row in range(FRAMES)])


def block(latents, w_in, w_time, w_first, w_second):
    row = lax.axis_index("rows").astype(jnp.int32)
    at = jnp.stack([row, lax.axis_index("section").astype(jnp.int32)])
    half = lax.dynamic_slice_in_dim(w_first, row % 2 * 256, 256, 2)
    left = move_y(half, 1)
    right = move_y(half, -1)
    packed = pl.pallas_call(
        pack_kernel,
        out_shape=jax.ShapeDtypeStruct((FRAMES, 1, MSG), BF16),
        in_specs=[VM],
        out_specs=VM,
        scratch_shapes=[pltpu.VMEM((MSG, LF), F32)],
    )(latents.transpose(0, 3, 2, 1).reshape(CLIPS * LOCAL, LATC, LF))
    recv = lax.all_to_all(packed, "rows", split_axis=0, concat_axis=0, tiled=True)
    far_left = move_y(left[:, :, :128], 1)
    far_right = move_y(right[:, :, 128:], -1)
    far = jnp.concatenate([far_left, far_right], axis=2)
    left_swap = swap(left)
    right_swap = swap(right)
    far_swap = swap(far)
    taps = jnp.pad(w_in.reshape(3 * LATC, CH), ((0, 4), (0, 0)))
    x, h, mid, side = pl.pallas_call(
        first_kernel,
        out_shape=[
            jax.ShapeDtypeStruct((CELLS, CH), BF16),
            jax.ShapeDtypeStruct((CELLS, CH), BF16),
            jax.ShapeDtypeStruct((CELLS, 128), BF16),
            jax.ShapeDtypeStruct((CELLS, 256), BF16),
        ],
        in_specs=[SM] + [VM] * 8,
        out_specs=[VM] * 4,
        scratch_shapes=[
            pltpu.VMEM((CELLS, CH), BF16),
            pltpu.VMEM((2, CELLS, CH), BF16),
            pltpu.VMEM((CELLS, 384), F32),
            pltpu.VMEM((CELLS, 128), BF16),
            pltpu.VMEM((CELLS, 768), F32),
            pltpu.VMEM((CELLS, 256), BF16),
        ],
    )(at, recv, taps, w_time, w_first, left, right, left_swap, right_swap)
    out = pl.pallas_call(
        second_kernel,
        out_shape=jax.ShapeDtypeStruct((HS, W, 128), BF16),
        in_specs=[SM] + [VM] * 7,
        out_specs=VM,
        scratch_shapes=[
            pltpu.VMEM((CELLS, 384), F32),
            pltpu.VMEM((CELLS, 128), BF16),
            pltpu.VMEM((CELLS, 128), BF16),
            pltpu.VMEM((CELLS, CH), BF16),
        ],
    )(at, x, h, mid, side, far, far_swap, w_second)
    return out.reshape(1, HS, W, 128)


def solution(mesh):
    in_specs = (
        P(None, None, None, "rows"),
        P(),
        P(),
        P(None, None, None, "section"),
        P(None, None, None, "section"),
    )
    out_specs = P("rows", None, None, "section")
    return jax.shard_map(block, mesh=mesh, in_specs=in_specs, out_specs=out_specs, check_vma=False)
```

```python
import jax
import jax.numpy as jnp
from jax import lax
from jax.experimental import pallas as pl
from jax.experimental.pallas import tpu as pltpu
from jax.sharding import PartitionSpec as P


CH = 512
LATC = 4
HS = 4
W = 160
CELLS = HS * W
CLIPS = 4
LF = 8
UPS = 4
FRAMES = 128
GROUP = 16
LOCAL = 5
WINDOW = 4
MSG = LOCAL * WINDOW * LATC
STEP = 128

F32 = jnp.float32
BF16 = jnp.bfloat16


def dot(a, b):
    return jnp.dot(a, b, preferred_element_type=F32)


def iota(shape, dim):
    return lax.broadcasted_iota(jnp.int32, shape, dim)


def onehot(cond):
    return jnp.where(cond, 1.0, 0.0).astype(BF16)


def silu(t):
    return 0.5 * t * (1.0 + jnp.tanh(0.5 * t))


def pack_kernel(lat_ref, w_ref, out_ref, half_ref, flat_ref, sem):
    core = lax.axis_index("rows") % 2
    lanes = pl.ds(pl.multiple_of(core * 256, 256), 256)
    cut = pltpu.make_async_copy(w_ref.at[:, :, lanes, :], half_ref, sem)
    cut.start()
    for n in range(CLIPS * LOCAL):
        flat_ref[n * LATC : (n + 1) * LATC, :] = lat_ref[n].astype(F32)
    flat = flat_ref[...].astype(BF16)
    frame = iota((FRAMES, LF), 0)
    latent = iota((FRAMES, LF), 1)
    same_clip = iota((FRAMES, MSG), 0) // 32 == iota((FRAMES, MSG), 1) // (LOCAL * LATC)
    src = iota((MSG, MSG), 0) % (LOCAL * LATC)
    lane = iota((MSG, MSG), 1)
    home = (src // LATC == lane // 16) & (src % LATC == lane % LATC)
    total = jnp.zeros((FRAMES, MSG), F32)
    for j in range(WINDOW):
        pick = onehot(latent == jnp.maximum((frame % 32) // UPS - 3 + j, 0))
        taken = lax.dot_general(pick, flat, (((1,), (1,)), ((), ())), preferred_element_type=F32)
        taken = jnp.where(same_clip, taken, 0.0).astype(BF16)
        total = total + dot(taken, onehot(home & ((lane // LATC) % WINDOW == j)))
    out_ref[:, 0, :] = total.astype(BF16)
    cut.wait()


def loop(body, rows=CELLS, step=STEP):
    def wrapped(i, carry):
        return body(pl.ds(pl.multiple_of(i * step, step), step), carry)

    return wrapped, rows // step


def group_total(sums):
    lane = iota(sums.shape, 1)
    width = sums.shape[1]
    for d in (1, 2, 4, 8):
        up = pltpu.roll(sums, d, 1)
        down = pltpu.roll(sums, width - d, 1)
        sums = sums + jnp.where((lane & d) != 0, up, down)
    return sums


def norm_silu(src_ref, dst_ref, width):
    count = float(CELLS * GROUP)

    def add(rows, carry):
        return carry + jnp.sum(src_ref[rows, :].astype(F32).reshape(STEP // 8, 8, width), axis=0)

    def total(fn):
        body, n = loop(fn)
        part = lax.fori_loop(0, n, body, jnp.zeros((8, width), F32))
        part = jnp.sum(part, axis=0, keepdims=True)
        return group_total(jnp.broadcast_to(part, (8, width)))[:1] / count

    mean = total(add)

    def add_sq(rows, carry):
        t = src_ref[rows, :].astype(F32) - mean
        return carry + jnp.sum((t * t).reshape(STEP // 8, 8, width), axis=0)

    scale = lax.rsqrt(total(add_sq) + 1e-06)

    def write(rows, carry):
        t = (src_ref[rows, :].astype(F32) - mean) * scale
        dst_ref[rows, :] = silu(t).astype(BF16)
        return carry

    body, n = loop(write)
    lax.fori_loop(0, n, body, 0)


def conv(h_ref, weights, acc_ref):
    for dy in (1, 0, 2):
        src = slice(W, CELLS) if dy == 2 else slice(0, CELLS - W) if dy == 0 else slice(0, CELLS)
        dst = slice(W, CELLS) if dy == 0 else slice(0, CELLS - W) if dy == 2 else slice(0, CELLS)
        w = jnp.concatenate([ref[dy, dx] for ref in weights for dx in range(3)], axis=1)
        if dy == 1:
            acc_ref[...] = dot(h_ref[src, :], w)
        else:
            acc_ref[dst, :] += dot(h_ref[src, :], w)


def gathered(acc_ref, i, base=0):
    rows = slice(i * W, (i + 1) * W)
    col = iota((W, 128), 0)
    left = jnp.where(col == 0, 0.0, pltpu.roll(acc_ref[rows, base : base + 128], 1, 0))
    right = jnp.where(col == W - 1, 0.0, pltpu.roll(acc_ref[rows, base + 256 : base + 384], W - 1, 0))
    return left + acc_ref[rows, base + 128 : base + 256] + right


def quarter_of(section, slot):
    return section ^ (0, 1, 3, 2)[slot]


def main_kernel(recv_ref, w_in_ref, w_time_hbm, own_hbm, pair_hbm, pair_swap_hbm, cross_hbm, cross_swap_hbm,
                far_hbm, far_swap_hbm, w_second_hbm, out_ref,
                w_time_ref, inner_ref, outer_ref, taps_ref, u_ref, v_ref, x_ref, h_ref, wide_ref, h1_ref,
                all_ref, acc_ref, sems):
    row = lax.axis_index("rows").astype(jnp.int32)
    section = lax.axis_index("section").astype(jnp.int32)
    core = row % 2
    mine = pl.ds(pl.multiple_of(core * 256, 256), 256)
    other = pl.ds(pl.multiple_of(256 - core * 256, 256), 256)
    copies = [
        pltpu.make_async_copy(w_time_hbm, w_time_ref, sems.at[0]),
        pltpu.make_async_copy(own_hbm, inner_ref.at[0], sems.at[1]),
        pltpu.make_async_copy(pair_hbm, inner_ref.at[1, :, :, mine, :], sems.at[2]),
        pltpu.make_async_copy(pair_swap_hbm, inner_ref.at[1, :, :, other, :], sems.at[3]),
        pltpu.make_async_copy(cross_hbm, inner_ref.at[2, :, :, mine, :], sems.at[4]),
        pltpu.make_async_copy(cross_swap_hbm, inner_ref.at[2, :, :, other, :], sems.at[5]),
        pltpu.make_async_copy(far_hbm, inner_ref.at[3, :, :, mine, :], sems.at[6]),
        pltpu.make_async_copy(far_swap_hbm, inner_ref.at[3, :, :, other, :], sems.at[7]),
    ]
    for slot in range(4):
        lanes = pl.ds(pl.multiple_of(quarter_of(section, slot) * 128, 128), 128)
        copies.append(
            pltpu.make_async_copy(
                w_second_hbm.at[:, :, lanes, :], outer_ref.at[:, :, slot * 128 : (slot + 1) * 128, :], sems.at[8 + slot]
            )
        )
    for copy in copies:
        copy.start()

    taps_ref[...] = jnp.zeros_like(taps_ref)
    for k in range(3):
        taps_ref[k * LATC : (k + 1) * LATC, :] = w_in_ref[k].astype(F32)
    taps = taps_ref[...].astype(BF16)
    src = iota((CELLS, FRAMES), 1)
    at = iota((CELLS, FRAMES), 0)
    spread = dot(onehot((at >= src * LOCAL) & (at < src * LOCAL + LOCAL)), recv_ref[:, 0, :])
    lane = iota((CELLS, MSG), 1)
    own = iota((CELLS, MSG), 0) % LOCAL == lane // 16
    spread = jnp.where(own, spread, 0.0).astype(BF16)
    slot = iota((MSG, 16), 0) % 16
    col = iota((MSG, 16), 1)
    for s in range(2):
        picked = dot(spread, onehot(slot == col + s * LATC)).astype(BF16)
        u = dot(picked, taps).astype(BF16)
        if s == 1:
            u_ref[...] = u
        v_ref[s] = silu(u.astype(F32)).astype(BF16)
    sub = row % UPS
    total = u_ref[...].astype(F32)
    copies[0].wait()
    for k in range(3):
        which = (sub >= 2 - k).astype(jnp.int32)
        total = total + dot(v_ref[which], w_time_ref[k])
    x_ref[...] = total.astype(BF16)
    norm_silu(x_ref, h_ref, CH)
    for two in range(2):
        for copy in copies[1:4] if two == 0 else copies[4:8]:
            copy.wait()
        conv(h_ref, [inner_ref.at[2 * two], inner_ref.at[2 * two + 1]], wide_ref)
        for n in range(2):
            for i in range(HS):
                h1_ref[i * W : (i + 1) * W, n * 128 : (n + 1) * 128] = gathered(wide_ref, i, n * 384).astype(BF16)
        norm_silu(h1_ref, all_ref.at[:, two * 256 : (two + 1) * 256], 256)
    for copy in copies[8:]:
        copy.wait()
    conv(all_ref, [outer_ref], acc_ref)
    lanes = pl.ds(pl.multiple_of(section * 128, 128), 128)
    for i in range(HS):
        residual = x_ref[i * W : (i + 1) * W, lanes].astype(F32)
        out_ref[i] = (residual + gathered(acc_ref, i)).astype(BF16)


VM = pl.BlockSpec(memory_space=pltpu.VMEM)
HB = pl.BlockSpec(memory_space=pl.ANY)


def trade(value, across):
    pairs = []
    for row in range(FRAMES):
        for section in range(4):
            y = 4 * (row // 2 % 2) + section
            y = (((y + 1) ^ 1) - 1) % 8 if across else y ^ 1
            there = row // 4 * 4 + y // 4 * 2 + row % 2
            pairs.append((section * FRAMES + row, y % 4 * FRAMES + there))
    return lax.ppermute(value, ("section", "rows"), pairs)


def swap(value):
    return lax.ppermute(value, "rows", [(row, row ^ 1) for row in range(FRAMES)])


def block(latents, w_in, w_time, w_first, w_second):
    packed, half = pl.pallas_call(
        pack_kernel,
        out_shape=[
            jax.ShapeDtypeStruct((FRAMES, 1, MSG), BF16),
            jax.ShapeDtypeStruct((3, 3, 256, 128), BF16),
        ],
        in_specs=[VM, HB],
        out_specs=[VM, HB],
        scratch_shapes=[pltpu.VMEM((MSG, LF), F32), pltpu.SemaphoreType.DMA],
    )(latents.transpose(0, 3, 2, 1).reshape(CLIPS * LOCAL, LATC, LF), w_first)
    pair = trade(half, False)
    cross = trade(half, True)
    recv = lax.all_to_all(packed, "rows", split_axis=0, concat_axis=0, tiled=True)
    far_pair = trade(cross[:, :, :128], False)
    far_cross = trade(pair[:, :, 128:], True)
    pair_swap = swap(pair)
    cross_swap = swap(cross)
    far = jnp.concatenate([far_pair, far_cross], axis=2)
    far_swap = swap(far)
    out = pl.pallas_call(
        main_kernel,
        out_shape=jax.ShapeDtypeStruct((HS, W, 128), BF16),
        in_specs=[VM, VM] + [HB] * 9,
        out_specs=VM,
        scratch_shapes=[
            pltpu.VMEM((3, CH, CH), BF16),
            pltpu.VMEM((4, 3, 3, CH, 128), BF16),
            pltpu.VMEM((3, 3, CH, 128), BF16),
            pltpu.VMEM((16, CH), F32),
            pltpu.VMEM((CELLS, CH), BF16),
            pltpu.VMEM((2, CELLS, CH), BF16),
            pltpu.VMEM((CELLS, CH), BF16),
            pltpu.VMEM((CELLS, CH), BF16),
            pltpu.VMEM((CELLS, 768), F32),
            pltpu.VMEM((CELLS, 256), BF16),
            pltpu.VMEM((CELLS, CH), BF16),
            pltpu.VMEM((CELLS, 384), F32),
            pltpu.SemaphoreType.DMA((12,)),
        ],
    )(recv, w_in, w_time, w_first, pair, pair_swap, cross, cross_swap, far, far_swap, w_second)
    return out.reshape(1, HS, W, 128)


def solution(mesh):
    in_specs = (
        P(None, None, None, "rows"),
        P(),
        P(),
        P(None, None, None, "section"),
        P(None, None, None, "section"),
    )
    out_specs = P("rows", None, None, "section")
    return jax.shard_map(block, mesh=mesh, in_specs=in_specs, out_specs=out_specs, check_vma=False)
```

```python
import jax
import jax.numpy as jnp
from jax import lax
from jax.experimental import pallas as pl
from jax.experimental.pallas import tpu as pltpu
from jax.sharding import PartitionSpec as P


CH = 512
LATC = 4
HS = 4
W = 160
CELLS = HS * W
CLIPS = 4
LF = 8
UPS = 4
FRAMES = 128
PEERS = 64
GROUP = 16
LOCAL = 5
WINDOW = 4
MSG = LOCAL * WINDOW * LATC
STEP = 128

F32 = jnp.float32
BF16 = jnp.bfloat16


def dot(a, b):
    return jnp.dot(a, b, preferred_element_type=F32)


def iota(shape, dim):
    return lax.broadcasted_iota(jnp.int32, shape, dim)


def onehot(cond):
    return jnp.where(cond, 1.0, 0.0).astype(BF16)


def silu(t):
    return 0.5 * t * (1.0 + jnp.tanh(0.5 * t))


def pack_kernel(lat_ref, w_ref, out_ref, half_ref, flat_ref, sem):
    core = lax.axis_index("rows") % 2
    lanes = pl.ds(pl.multiple_of(core * 256, 256), 256)
    cut = pltpu.make_async_copy(w_ref.at[:, :, lanes, :], half_ref, sem)
    cut.start()
    for n in range(CLIPS * LOCAL):
        flat_ref[n * LATC : (n + 1) * LATC, :] = lat_ref[n].astype(F32)
    flat = flat_ref[...].astype(BF16)
    peer = iota((PEERS, LF), 0)
    latent = iota((PEERS, LF), 1)
    same_clip = iota((PEERS, MSG), 0) // 16 == iota((PEERS, MSG), 1) // (LOCAL * LATC)
    src = iota((MSG, MSG), 0) % (LOCAL * LATC)
    lane = iota((MSG, MSG), 1)
    home = (src // LATC == lane // 16) & (src % LATC == lane % LATC)
    total = jnp.zeros((PEERS, MSG), F32)
    for j in range(WINDOW):
        pick = onehot(latent == jnp.maximum(peer % 16 // 2 - 3 + j, 0))
        taken = lax.dot_general(pick, flat, (((1,), (1,)), ((), ())), preferred_element_type=F32)
        taken = jnp.where(same_clip, taken, 0.0).astype(BF16)
        total = total + dot(taken, onehot(home & ((lane // LATC) % WINDOW == j)))
    out_ref[:, 0, :] = total.astype(BF16)
    cut.wait()


def loop(body, rows=CELLS, step=STEP):
    def wrapped(i, carry):
        return body(pl.ds(pl.multiple_of(i * step, step), step), carry)

    return wrapped, rows // step


def group_total(sums):
    lane = iota(sums.shape, 1)
    width = sums.shape[1]
    for d in (1, 2, 4, 8):
        up = pltpu.roll(sums, d, 1)
        down = pltpu.roll(sums, width - d, 1)
        sums = sums + jnp.where((lane & d) != 0, up, down)
    return sums


def norm_silu(src_ref, dst_ref, width):
    count = float(CELLS * GROUP)

    def add(rows, carry):
        return carry + jnp.sum(src_ref[rows, :].astype(F32).reshape(STEP // 8, 8, width), axis=0)

    def total(fn):
        body, n = loop(fn)
        part = lax.fori_loop(0, n, body, jnp.zeros((8, width), F32))
        part = jnp.sum(part, axis=0, keepdims=True)
        return group_total(jnp.broadcast_to(part, (8, width)))[:1] / count

    mean = total(add)

    def add_sq(rows, carry):
        t = src_ref[rows, :].astype(F32) - mean
        return carry + jnp.sum((t * t).reshape(STEP // 8, 8, width), axis=0)

    scale = lax.rsqrt(total(add_sq) + 1e-06)

    def write(rows, carry):
        t = (src_ref[rows, :].astype(F32) - mean) * scale
        dst_ref[rows, :] = silu(t).astype(BF16)
        return carry

    body, n = loop(write)
    lax.fori_loop(0, n, body, 0)


def conv(h_ref, weights, acc_ref):
    for dy in (1, 0, 2):
        src = slice(W, CELLS) if dy == 2 else slice(0, CELLS - W) if dy == 0 else slice(0, CELLS)
        dst = slice(W, CELLS) if dy == 0 else slice(0, CELLS - W) if dy == 2 else slice(0, CELLS)
        w = jnp.concatenate([ref[dy, dx] for ref in weights for dx in range(3)], axis=1)
        if dy == 1:
            acc_ref[...] = dot(h_ref[src, :], w)
        else:
            acc_ref[dst, :] += dot(h_ref[src, :], w)


def gathered(acc_ref, i, base=0):
    rows = slice(i * W, (i + 1) * W)
    col = iota((W, 128), 0)
    left = jnp.where(col == 0, 0.0, pltpu.roll(acc_ref[rows, base : base + 128], 1, 0))
    right = jnp.where(col == W - 1, 0.0, pltpu.roll(acc_ref[rows, base + 256 : base + 384], W - 1, 0))
    return left + acc_ref[rows, base + 128 : base + 256] + right


def halves(core):
    mine = pl.ds(pl.multiple_of(core * 256, 256), 256)
    other = pl.ds(pl.multiple_of(256 - core * 256, 256), 256)
    return mine, other


def start_all(pairs, sems):
    copies = [pltpu.make_async_copy(src, dst, sems.at[n]) for n, (src, dst) in enumerate(pairs)]
    for copy in copies:
        copy.start()
    return copies


def my_place():
    return lax.axis_index("rows").astype(jnp.int32), lax.axis_index("section").astype(jnp.int32)


def inner_quarters(h_ref, weights, acc_ref, h1_ref, dst_ref):
    conv(h_ref, weights, acc_ref)
    for n in range(len(weights)):
        for i in range(HS):
            h1_ref[i * W : (i + 1) * W, n * 128 : (n + 1) * 128] = gathered(acc_ref, i, n * 384).astype(BF16)
    norm_silu(h1_ref, dst_ref, len(weights) * 128)


def first_kernel(recv_ref, w_in_ref, w_time_hbm, cross_hbm, cross_swap_hbm, x_own_ref, h_ref, h2_ref,
                 w_time_ref, inner_ref, taps_ref, u_ref, v_ref, x_ref, acc_ref, h1_ref, sems):
    row, section = my_place()
    mine, other = halves(row % 2)
    copies = start_all(
        [
            (w_time_hbm, w_time_ref),
            (cross_hbm, inner_ref.at[:, :, mine, :]),
            (cross_swap_hbm, inner_ref.at[:, :, other, :]),
        ],
        sems,
    )
    taps_ref[...] = jnp.zeros_like(taps_ref)
    for k in range(3):
        taps_ref[k * LATC : (k + 1) * LATC, :] = w_in_ref[k].astype(F32)
    taps = taps_ref[...].astype(BF16)
    got = iota((CELLS, FRAMES), 1)
    src = got % PEERS * 2 + got // PEERS
    at = iota((CELLS, FRAMES), 0)
    spread = dot(onehot((at >= src * LOCAL) & (at < src * LOCAL + LOCAL)), recv_ref[...])
    lane = iota((CELLS, MSG), 1)
    own = iota((CELLS, MSG), 0) % LOCAL == lane // 16
    spread = jnp.where(own, spread, 0.0).astype(BF16)
    slot = iota((MSG, 16), 0) % 16
    col = iota((MSG, 16), 1)
    for s in range(2):
        picked = dot(spread, onehot(slot == col + s * LATC)).astype(BF16)
        u = dot(picked, taps).astype(BF16)
        if s == 1:
            u_ref[...] = u
        v_ref[s] = silu(u.astype(F32)).astype(BF16)
    sub = row % UPS
    total = u_ref[...].astype(F32)
    copies[0].wait()
    for k in range(3):
        which = (sub >= 2 - k).astype(jnp.int32)
        total = total + dot(v_ref[which], w_time_ref[k])
    x_ref[...] = total.astype(BF16)
    x_own_ref[...] = x_ref[:, pl.ds(pl.multiple_of(section * 128, 128), 128)]
    norm_silu(x_ref, h_ref, CH)
    copies[1].wait()
    copies[2].wait()
    inner_quarters(h_ref, [inner_ref], acc_ref, h1_ref, h2_ref)


def second_kernel(x_own_ref, h_hbm, cross_h2_ref, own_hbm, pair_hbm, pair_swap_hbm, w_hbm, out_ref,
                  h_ref, inner_ref, outer_ref, wide_ref, h1_ref, all_ref, acc_ref, sems):
    row, section = my_place()
    mine, other = halves(row % 2)
    pairs = [
        (h_hbm, h_ref),
        (own_hbm, inner_ref.at[0]),
        (pair_hbm, inner_ref.at[1, :, :, mine, :]),
        (pair_swap_hbm, inner_ref.at[1, :, :, other, :]),
    ]
    for slot in range(3):
        lanes = pl.ds(pl.multiple_of((section ^ (0, 1, 3)[slot]) * 128, 128), 128)
        pairs.append((w_hbm.at[:, :, lanes, :], outer_ref.at[:, :, slot * 128 : (slot + 1) * 128, :]))
    copies = start_all(pairs, sems)
    all_ref[:, 256:] = cross_h2_ref[...]
    for copy in copies[:4]:
        copy.wait()
    inner_quarters(h_ref, [inner_ref.at[0], inner_ref.at[1]], wide_ref, h1_ref, all_ref.at[:, :256])
    for copy in copies[4:]:
        copy.wait()
    conv(all_ref, [outer_ref], acc_ref)
    for i in range(HS):
        rows = slice(i * W, (i + 1) * W)
        out_ref[rows, :] = x_own_ref[rows, :].astype(F32) + gathered(acc_ref, i)


def third_kernel(part_ref, far_ref, w_hbm, out_ref, outer_ref, acc_ref, sems):
    section = lax.axis_index("section").astype(jnp.int32)
    lanes = pl.ds(pl.multiple_of((section ^ 2) * 128, 128), 128)
    for copy in start_all([(w_hbm.at[:, :, lanes, :], outer_ref)], sems):
        copy.wait()
    conv(far_ref, [outer_ref], acc_ref)
    for i in range(HS):
        out_ref[i] = (part_ref[i * W : (i + 1) * W, :] + gathered(acc_ref, i)).astype(BF16)


VM = pl.BlockSpec(memory_space=pltpu.VMEM)
HB = pl.BlockSpec(memory_space=pl.ANY)


def trade(value, across):
    pairs = []
    for row in range(FRAMES):
        for section in range(4):
            y = 4 * (row // 2 % 2) + section
            y = (((y + 1) ^ 1) - 1) % 8 if across else y ^ 1
            there = row // 4 * 4 + y // 4 * 2 + row % 2
            pairs.append((section * FRAMES + row, y % 4 * FRAMES + there))
    return lax.ppermute(value, ("section", "rows"), pairs)


def swap(value):
    return lax.ppermute(value, "rows", [(row, row ^ 1) for row in range(FRAMES)])


def block(latents, w_in, w_time, w_first, w_second):
    packed, half = pl.pallas_call(
        pack_kernel,
        out_shape=[
            jax.ShapeDtypeStruct((PEERS, 1, MSG), BF16),
            jax.ShapeDtypeStruct((3, 3, 256, 128), BF16),
        ],
        in_specs=[VM, HB],
        out_specs=[VM, VM],
        scratch_shapes=[pltpu.VMEM((MSG, LF), F32), pltpu.SemaphoreType.DMA],
    )(latents.transpose(0, 3, 2, 1).reshape(CLIPS * LOCAL, LATC, LF), w_first)
    cross = trade(half, True)
    pair = trade(half, False)
    same_core = [list(range(core, FRAMES, 2)) for core in range(2)]
    got = lax.all_to_all(packed, "rows", split_axis=0, concat_axis=0, axis_index_groups=same_core, tiled=True)
    cores = [[row, row + 1] for row in range(0, FRAMES, 2)]
    recv = lax.all_gather(got.reshape(PEERS, MSG), "rows", axis=0, axis_index_groups=cores, tiled=True)
    cross_swap = swap(cross)
    pair_swap = swap(pair)
    x_own, h, cross_h2 = pl.pallas_call(
        first_kernel,
        out_shape=[
            jax.ShapeDtypeStruct((CELLS, 128), BF16),
            jax.ShapeDtypeStruct((CELLS, CH), BF16),
            jax.ShapeDtypeStruct((CELLS, 128), BF16),
        ],
        in_specs=[VM, VM] + [HB] * 3,
        out_specs=[VM] * 3,
        scratch_shapes=[
            pltpu.VMEM((3, CH, CH), BF16),
            pltpu.VMEM((3, 3, CH, 128), BF16),
            pltpu.VMEM((16, CH), F32),
            pltpu.VMEM((CELLS, CH), BF16),
            pltpu.VMEM((2, CELLS, CH), BF16),
            pltpu.VMEM((CELLS, CH), BF16),
            pltpu.VMEM((CELLS, 384), F32),
            pltpu.VMEM((CELLS, 128), BF16),
            pltpu.SemaphoreType.DMA((3,)),
        ],
    )(recv, w_in, w_time, cross, cross_swap)
    far = trade(cross_h2, False)
    part = pl.pallas_call(
        second_kernel,
        out_shape=jax.ShapeDtypeStruct((CELLS, 128), F32),
        in_specs=[VM, HB, VM] + [HB] * 4,
        out_specs=VM,
        scratch_shapes=[
            pltpu.VMEM((CELLS, CH), BF16),
            pltpu.VMEM((2, 3, 3, CH, 128), BF16),
            pltpu.VMEM((3, 3, 384, 128), BF16),
            pltpu.VMEM((CELLS, 768), F32),
            pltpu.VMEM((CELLS, 256), BF16),
            pltpu.VMEM((CELLS, 384), BF16),
            pltpu.VMEM((CELLS, 384), F32),
            pltpu.SemaphoreType.DMA((7,)),
        ],
    )(x_own, h, cross_h2, w_first, pair, pair_swap, w_second)
    out = pl.pallas_call(
        third_kernel,
        out_shape=jax.ShapeDtypeStruct((HS, W, 128), BF16),
        in_specs=[VM, VM, HB],
        out_specs=VM,
        scratch_shapes=[
            pltpu.VMEM((3, 3, 128, 128), BF16),
            pltpu.VMEM((CELLS, 384), F32),
            pltpu.SemaphoreType.DMA((1,)),
        ],
    )(part, far, w_second)
    return out.reshape(1, HS, W, 128)


def solution(mesh):
    in_specs = (
        P(None, None, None, "rows"),
        P(),
        P(),
        P(None, None, None, "section"),
        P(None, None, None, "section"),
    )
    out_specs = P("rows", None, None, "section")
    return jax.shard_map(block, mesh=mesh, in_specs=in_specs, out_specs=out_specs, check_vma=False)
```

```python
import jax
import jax.numpy as jnp
from jax import lax
from jax.experimental import pallas as pl
from jax.experimental.pallas import tpu as pltpu
from jax.sharding import PartitionSpec as P


CH = 512
LATC = 4
HS = 4
W = 160
CELLS = HS * W
CLIPS = 4
LF = 8
UPS = 4
FRAMES = 128
PEERS = 64
GROUP = 16
LOCAL = 5
WINDOW = 4
MSG = LOCAL * WINDOW * LATC
STEP = 128

F32 = jnp.float32
BF16 = jnp.bfloat16


def dot(a, b):
    return jnp.dot(a, b, preferred_element_type=F32)


def iota(shape, dim):
    return lax.broadcasted_iota(jnp.int32, shape, dim)


def onehot(cond):
    return jnp.where(cond, 1.0, 0.0).astype(BF16)


def silu(t):
    return 0.5 * t * (1.0 + jnp.tanh(0.5 * t))


def pack_kernel(lat_ref, w_ref, out_ref, half_ref, flat_ref, sem):
    core = lax.axis_index("rows") % 2
    lanes = pl.ds(pl.multiple_of(core * 256, 256), 256)
    cut = pltpu.make_async_copy(w_ref.at[:, :, lanes, :], half_ref, sem)
    cut.start()
    for n in range(CLIPS * LOCAL):
        flat_ref[n * LATC : (n + 1) * LATC, :] = lat_ref[n].astype(F32)
    flat = flat_ref[...].astype(BF16)
    peer = iota((PEERS, LF), 0)
    latent = iota((PEERS, LF), 1)
    same_clip = iota((PEERS, MSG), 0) // 16 == iota((PEERS, MSG), 1) // (LOCAL * LATC)
    src = iota((MSG, MSG), 0) % (LOCAL * LATC)
    lane = iota((MSG, MSG), 1)
    home = (src // LATC == lane // 16) & (src % LATC == lane % LATC)
    total = jnp.zeros((PEERS, MSG), F32)
    for j in range(WINDOW):
        pick = onehot(latent == jnp.maximum(peer % 16 // 2 - 3 + j, 0))
        taken = lax.dot_general(pick, flat, (((1,), (1,)), ((), ())), preferred_element_type=F32)
        taken = jnp.where(same_clip, taken, 0.0).astype(BF16)
        total = total + dot(taken, onehot(home & ((lane // LATC) % WINDOW == j)))
    out_ref[:, 0, :] = total.astype(BF16)
    cut.wait()


def loop(body, rows=CELLS, step=STEP):
    def wrapped(i, carry):
        return body(pl.ds(pl.multiple_of(i * step, step), step), carry)

    return wrapped, rows // step


def group_total(sums):
    lane = iota(sums.shape, 1)
    width = sums.shape[1]
    for d in (1, 2, 4, 8):
        up = pltpu.roll(sums, d, 1)
        down = pltpu.roll(sums, width - d, 1)
        sums = sums + jnp.where((lane & d) != 0, up, down)
    return sums


def norm_silu(src_ref, dst_ref, width):
    count = float(CELLS * GROUP)

    def add(rows, carry):
        return carry + jnp.sum(src_ref[rows, :].astype(F32).reshape(STEP // 8, 8, width), axis=0)

    def total(fn):
        body, n = loop(fn)
        part = lax.fori_loop(0, n, body, jnp.zeros((8, width), F32))
        part = jnp.sum(part, axis=0, keepdims=True)
        return group_total(jnp.broadcast_to(part, (8, width)))[:1] / count

    mean = total(add)

    def add_sq(rows, carry):
        t = src_ref[rows, :].astype(F32) - mean
        return carry + jnp.sum((t * t).reshape(STEP // 8, 8, width), axis=0)

    scale = lax.rsqrt(total(add_sq) + 1e-06)

    def write(rows, carry):
        t = (src_ref[rows, :].astype(F32) - mean) * scale
        dst_ref[rows, :] = silu(t).astype(BF16)
        return carry

    body, n = loop(write)
    lax.fori_loop(0, n, body, 0)


def conv(h_ref, weights, acc_ref):
    for dy in (1, 0, 2):
        src = slice(W, CELLS) if dy == 2 else slice(0, CELLS - W) if dy == 0 else slice(0, CELLS)
        dst = slice(W, CELLS) if dy == 0 else slice(0, CELLS - W) if dy == 2 else slice(0, CELLS)
        w = jnp.concatenate([ref[dy, dx] for ref in weights for dx in range(3)], axis=1)
        if dy == 1:
            acc_ref[...] = dot(h_ref[src, :], w)
        else:
            acc_ref[dst, :] += dot(h_ref[src, :], w)


def gathered(acc_ref, i, base=0):
    rows = slice(i * W, (i + 1) * W)
    col = iota((W, 128), 0)
    left = jnp.where(col == 0, 0.0, pltpu.roll(acc_ref[rows, base : base + 128], 1, 0))
    right = jnp.where(col == W - 1, 0.0, pltpu.roll(acc_ref[rows, base + 256 : base + 384], W - 1, 0))
    return left + acc_ref[rows, base + 128 : base + 256] + right


def halves(core):
    mine = pl.ds(pl.multiple_of(core * 256, 256), 256)
    other = pl.ds(pl.multiple_of(256 - core * 256, 256), 256)
    return mine, other


def start_all(pairs, sems):
    copies = [pltpu.make_async_copy(src, dst, sems.at[n]) for n, (src, dst) in enumerate(pairs)]
    for copy in copies:
        copy.start()
    return copies


def my_place():
    return lax.axis_index("rows").astype(jnp.int32), lax.axis_index("section").astype(jnp.int32)


def inner_quarters(h_ref, weights, acc_ref, h1_ref, dst_ref):
    conv(h_ref, weights, acc_ref)
    for n in range(len(weights)):
        for i in range(HS):
            h1_ref[i * W : (i + 1) * W, n * 128 : (n + 1) * 128] = gathered(acc_ref, i, n * 384).astype(BF16)
    norm_silu(h1_ref, dst_ref, len(weights) * 128)


def first_kernel(recv_ref, w_in_ref, w_time_hbm, own_hbm, cross_hbm, cross_swap_hbm, x_own_ref, h2_ref,
                 w_time_ref, inner_ref, taps_ref, u_ref, v_ref, x_ref, h_ref, acc_ref, h1_ref, sems):
    row, section = my_place()
    mine, other = halves(row % 2)
    copies = start_all(
        [
            (w_time_hbm, w_time_ref),
            (own_hbm, inner_ref.at[0]),
            (cross_hbm, inner_ref.at[1, :, :, mine, :]),
            (cross_swap_hbm, inner_ref.at[1, :, :, other, :]),
        ],
        sems,
    )
    taps_ref[...] = jnp.zeros_like(taps_ref)
    for k in range(3):
        taps_ref[k * LATC : (k + 1) * LATC, :] = w_in_ref[k].astype(F32)
    taps = taps_ref[...].astype(BF16)
    got = iota((CELLS, FRAMES), 1)
    src = got % PEERS * 2 + got // PEERS
    at = iota((CELLS, FRAMES), 0)
    spread = dot(onehot((at >= src * LOCAL) & (at < src * LOCAL + LOCAL)), recv_ref[...])
    lane = iota((CELLS, MSG), 1)
    own = iota((CELLS, MSG), 0) % LOCAL == lane // 16
    spread = jnp.where(own, spread, 0.0).astype(BF16)
    slot = iota((MSG, 16), 0) % 16
    col = iota((MSG, 16), 1)
    for s in range(2):
        picked = dot(spread, onehot(slot == col + s * LATC)).astype(BF16)
        u = dot(picked, taps).astype(BF16)
        if s == 1:
            u_ref[...] = u
        v_ref[s] = silu(u.astype(F32)).astype(BF16)
    sub = row % UPS
    total = u_ref[...].astype(F32)
    copies[0].wait()
    for k in range(3):
        which = (sub >= 2 - k).astype(jnp.int32)
        total = total + dot(v_ref[which], w_time_ref[k])
    x_ref[...] = total.astype(BF16)
    x_own_ref[...] = x_ref[:, pl.ds(pl.multiple_of(section * 128, 128), 128)]
    norm_silu(x_ref, h_ref, CH)
    for copy in copies[1:]:
        copy.wait()
    inner_quarters(h_ref, [inner_ref.at[0], inner_ref.at[1]], acc_ref, h1_ref, h2_ref)


def two_slots(w_hbm, outer_ref, slots):
    section = lax.axis_index("section").astype(jnp.int32)
    pairs = []
    for n, slot in enumerate(slots):
        lanes = pl.ds(pl.multiple_of((section ^ slot) * 128, 128), 128)
        pairs.append((w_hbm.at[:, :, lanes, :], outer_ref.at[:, :, n * 128 : (n + 1) * 128, :]))
    return pairs


def second_kernel(x_own_ref, h2_ref, w_hbm, out_ref, outer_ref, acc_ref, sems):
    for copy in start_all(two_slots(w_hbm, outer_ref, (0, 3)), sems):
        copy.wait()
    conv(h2_ref, [outer_ref], acc_ref)
    for i in range(HS):
        rows = slice(i * W, (i + 1) * W)
        out_ref[rows, :] = x_own_ref[rows, :].astype(F32) + gathered(acc_ref, i)


def third_kernel(part_ref, far_ref, w_hbm, out_ref, outer_ref, acc_ref, sems):
    for copy in start_all(two_slots(w_hbm, outer_ref, (1, 2)), sems):
        copy.wait()
    conv(far_ref, [outer_ref], acc_ref)
    for i in range(HS):
        out_ref[i] = (part_ref[i * W : (i + 1) * W, :] + gathered(acc_ref, i)).astype(BF16)


VM = pl.BlockSpec(memory_space=pltpu.VMEM)
HB = pl.BlockSpec(memory_space=pl.ANY)


def trade(value, across):
    pairs = []
    for row in range(FRAMES):
        for section in range(4):
            y = 4 * (row // 2 % 2) + section
            y = (((y + 1) ^ 1) - 1) % 8 if across else y ^ 1
            there = row // 4 * 4 + y // 4 * 2 + row % 2
            pairs.append((section * FRAMES + row, y % 4 * FRAMES + there))
    return lax.ppermute(value, ("section", "rows"), pairs)


def swap(value):
    return lax.ppermute(value, "rows", [(row, row ^ 1) for row in range(FRAMES)])


def block(latents, w_in, w_time, w_first, w_second):
    packed, half = pl.pallas_call(
        pack_kernel,
        out_shape=[
            jax.ShapeDtypeStruct((PEERS, 1, MSG), BF16),
            jax.ShapeDtypeStruct((3, 3, 256, 128), BF16),
        ],
        in_specs=[VM, HB],
        out_specs=[VM, VM],
        scratch_shapes=[pltpu.VMEM((MSG, LF), F32), pltpu.SemaphoreType.DMA],
    )(latents.transpose(0, 3, 2, 1).reshape(CLIPS * LOCAL, LATC, LF), w_first)
    cross = trade(half, True)
    same_core = [list(range(core, FRAMES, 2)) for core in range(2)]
    got = lax.all_to_all(packed, "rows", split_axis=0, concat_axis=0, axis_index_groups=same_core, tiled=True)
    cross_swap = swap(cross)
    got, cross_swap = lax.optimization_barrier((got.reshape(PEERS, MSG), cross_swap))
    cores = [[row, row + 1] for row in range(0, FRAMES, 2)]
    recv = lax.all_gather(got, "rows", axis=0, axis_index_groups=cores, tiled=True)
    x_own, h2 = pl.pallas_call(
        first_kernel,
        out_shape=[
            jax.ShapeDtypeStruct((CELLS, 128), BF16),
            jax.ShapeDtypeStruct((CELLS, 256), BF16),
        ],
        in_specs=[VM, VM] + [HB] * 4,
        out_specs=[VM] * 2,
        scratch_shapes=[
            pltpu.VMEM((3, CH, CH), BF16),
            pltpu.VMEM((2, 3, 3, CH, 128), BF16),
            pltpu.VMEM((16, CH), F32),
            pltpu.VMEM((CELLS, CH), BF16),
            pltpu.VMEM((2, CELLS, CH), BF16),
            pltpu.VMEM((CELLS, CH), BF16),
            pltpu.VMEM((CELLS, CH), BF16),
            pltpu.VMEM((CELLS, 768), F32),
            pltpu.VMEM((CELLS, 256), BF16),
            pltpu.SemaphoreType.DMA((4,)),
        ],
    )(recv, w_in, w_time, w_first, cross, cross_swap)
    far = trade(h2, False)
    weights = [
        pltpu.VMEM((3, 3, 256, 128), BF16),
        pltpu.VMEM((CELLS, 384), F32),
        pltpu.SemaphoreType.DMA((2,)),
    ]
    part = pl.pallas_call(
        second_kernel,
        out_shape=jax.ShapeDtypeStruct((CELLS, 128), F32),
        in_specs=[VM, VM, HB],
        out_specs=VM,
        scratch_shapes=weights,
        compiler_params=pltpu.CompilerParams(vmem_limit_bytes=67_000_000),
    )(x_own, h2, w_second)
    out = pl.pallas_call(
        third_kernel,
        out_shape=jax.ShapeDtypeStruct((HS, W, 128), BF16),
        in_specs=[VM, VM, HB],
        out_specs=VM,
        scratch_shapes=weights,
    )(part, far, w_second)
    return out.reshape(1, HS, W, 128)


def solution(mesh):
    in_specs = (
        P(None, None, None, "rows"),
        P(),
        P(),
        P(None, None, None, "section"),
        P(None, None, None, "section"),
    )
    out_specs = P("rows", None, None, "section")
    return jax.shard_map(block, mesh=mesh, in_specs=in_specs, out_specs=out_specs, check_vma=False)
```

```python
import jax
import jax.numpy as jnp
import numpy as np
from jax import lax
from jax.experimental import pallas as pl
from jax.experimental.pallas import tpu as pltpu
from jax.sharding import PartitionSpec as P


CH = 512
LATC = 4
HS = 4
W = 160
CELLS = HS * W
CLIPS = 4
LF = 8
UPS = 4
FRAMES = 128
GROUP = 16
LOCAL = 5
WINDOW = 4
MSG = LOCAL * WINDOW * LATC
STEP = 128

F32 = jnp.float32
BF16 = jnp.bfloat16


def dot(a, b):
    return jnp.dot(a, b, preferred_element_type=F32)


def iota(shape, dim):
    return lax.broadcasted_iota(jnp.int32, shape, dim)


def onehot(cond):
    return jnp.where(cond, 1.0, 0.0).astype(BF16)


def silu(t):
    return 0.5 * t * (1.0 + jnp.tanh(0.5 * t))


def pack_kernel(lat_ref, w_ref, out_ref, half_ref, flat_ref, sem):
    core = lax.axis_index("rows") % 2
    lanes = pl.ds(pl.multiple_of(core * 256, 256), 256)
    cut = pltpu.make_async_copy(w_ref.at[:, :, lanes, :], half_ref, sem)
    cut.start()
    for n in range(CLIPS * LOCAL):
        flat_ref[n * LATC : (n + 1) * LATC, :] = lat_ref[n].astype(F32)
    flat = flat_ref[...].astype(BF16)
    peer = iota((FRAMES, LF), 0)
    latent = iota((FRAMES, LF), 1)
    same_clip = iota((FRAMES, MSG), 0) // 32 == iota((FRAMES, MSG), 1) // (LOCAL * LATC)
    src = iota((MSG, MSG), 0) % (LOCAL * LATC)
    lane = iota((MSG, MSG), 1)
    home = (src // LATC == lane // 16) & (src % LATC == lane % LATC)
    total = jnp.zeros((FRAMES, MSG), F32)
    for j in range(WINDOW):
        pick = onehot(latent == jnp.maximum(peer % 32 // UPS - 3 + j, 0))
        taken = lax.dot_general(pick, flat, (((1,), (1,)), ((), ())), preferred_element_type=F32)
        taken = jnp.where(same_clip, taken, 0.0).astype(BF16)
        total = total + dot(taken, onehot(home & ((lane // LATC) % WINDOW == j)))
    out_ref[:, 0, :] = total.astype(BF16)
    cut.wait()


def loop(body, rows=CELLS, step=STEP):
    def wrapped(i, carry):
        return body(pl.ds(pl.multiple_of(i * step, step), step), carry)

    return wrapped, rows // step


def group_total(sums):
    lane = iota(sums.shape, 1)
    width = sums.shape[1]
    for d in (1, 2, 4, 8):
        up = pltpu.roll(sums, d, 1)
        down = pltpu.roll(sums, width - d, 1)
        sums = sums + jnp.where((lane & d) != 0, up, down)
    return sums


def norm_silu(src_ref, dst_ref, width):
    count = float(CELLS * GROUP)

    def add(rows, carry):
        return carry + jnp.sum(src_ref[rows, :].astype(F32).reshape(STEP // 8, 8, width), axis=0)

    def total(fn):
        body, n = loop(fn)
        part = lax.fori_loop(0, n, body, jnp.zeros((8, width), F32))
        part = jnp.sum(part, axis=0, keepdims=True)
        return group_total(jnp.broadcast_to(part, (8, width)))[:1] / count

    mean = total(add)

    def add_sq(rows, carry):
        t = src_ref[rows, :].astype(F32) - mean
        return carry + jnp.sum((t * t).reshape(STEP // 8, 8, width), axis=0)

    scale = lax.rsqrt(total(add_sq) + 1e-06)

    def write(rows, carry):
        t = (src_ref[rows, :].astype(F32) - mean) * scale
        dst_ref[rows, :] = silu(t).astype(BF16)
        return carry

    body, n = loop(write)
    lax.fori_loop(0, n, body, 0)


def conv(h_ref, weights, acc_ref):
    for dy in (1, 0, 2):
        src = slice(W, CELLS) if dy == 2 else slice(0, CELLS - W) if dy == 0 else slice(0, CELLS)
        dst = slice(W, CELLS) if dy == 0 else slice(0, CELLS - W) if dy == 2 else slice(0, CELLS)
        w = jnp.concatenate([ref[dy, dx] for ref in weights for dx in range(3)], axis=1)
        if dy == 1:
            acc_ref[...] = dot(h_ref[src, :], w)
        else:
            acc_ref[dst, :] += dot(h_ref[src, :], w)


def gathered(acc_ref, i, base=0):
    rows = slice(i * W, (i + 1) * W)
    col = iota((W, 128), 0)
    left = jnp.where(col == 0, 0.0, pltpu.roll(acc_ref[rows, base : base + 128], 1, 0))
    right = jnp.where(col == W - 1, 0.0, pltpu.roll(acc_ref[rows, base + 256 : base + 384], W - 1, 0))
    return left + acc_ref[rows, base + 128 : base + 256] + right


def halves(core):
    mine = pl.ds(pl.multiple_of(core * 256, 256), 256)
    other = pl.ds(pl.multiple_of(256 - core * 256, 256), 256)
    return mine, other


def start_all(pairs, sems):
    copies = [pltpu.make_async_copy(src, dst, sems.at[n]) for n, (src, dst) in enumerate(pairs)]
    for copy in copies:
        copy.start()
    return copies


def my_place():
    return lax.axis_index("rows").astype(jnp.int32), lax.axis_index("section").astype(jnp.int32)


def inner_quarters(h_ref, weights, acc_ref, h1_ref, dst_ref):
    conv(h_ref, weights, acc_ref)
    for n in range(len(weights)):
        for i in range(HS):
            h1_ref[i * W : (i + 1) * W, n * 128 : (n + 1) * 128] = gathered(acc_ref, i, n * 384).astype(BF16)
    norm_silu(h1_ref, dst_ref, len(weights) * 128)


def taps_kernel(w_in_ref, out_ref, taps_ref):
    taps_ref[...] = jnp.zeros_like(taps_ref)
    for k in range(3):
        taps_ref[k * LATC : (k + 1) * LATC, :] = w_in_ref[k].astype(F32)
    taps = taps_ref[...].astype(BF16)
    lane = iota((MSG, 16), 0) % 16
    tap = iota((MSG, 16), 1)
    for s in range(2):
        out_ref[:, s * CH : (s + 1) * CH] = dot(onehot(lane == tap + s * LATC), taps).astype(BF16)


def first_kernel(recv_ref, rows_of_cell_ref, lanes_of_cell_ref, taps_ref, w_time_hbm, own_hbm, cross_hbm, cross_swap_hbm, x_own_ref, h2_ref,
                 w_time_ref, inner_ref, u_ref, v_ref, x_ref, h_ref, acc_ref, h1_ref, sems):
    row, section = my_place()
    mine, other = halves(row % 2)
    copies = start_all(
        [
            (w_time_hbm, w_time_ref),
            (own_hbm, inner_ref.at[0]),
            (cross_hbm, inner_ref.at[1, :, :, mine, :]),
            (cross_swap_hbm, inner_ref.at[1, :, :, other, :]),
        ],
        sems,
    )
    spread = (dot(rows_of_cell_ref[...], recv_ref[:, 0, :]) * lanes_of_cell_ref[...]).astype(BF16)
    for s in range(2):
        u = dot(spread, taps_ref[:, s * CH : (s + 1) * CH]).astype(BF16)
        if s == 1:
            u_ref[...] = u
        v_ref[s] = silu(u.astype(F32)).astype(BF16)
    sub = row % UPS
    total = u_ref[...].astype(F32)
    copies[0].wait()
    for k in range(3):
        which = (sub >= 2 - k).astype(jnp.int32)
        total = total + dot(v_ref[which], w_time_ref[k])
    x_ref[...] = total.astype(BF16)
    x_own_ref[...] = x_ref[:, pl.ds(pl.multiple_of(section * 128, 128), 128)]
    norm_silu(x_ref, h_ref, CH)
    for copy in copies[1:]:
        copy.wait()
    inner_quarters(h_ref, [inner_ref.at[0], inner_ref.at[1]], acc_ref, h1_ref, h2_ref)


def two_slots(w_hbm, outer_ref, slots):
    section = lax.axis_index("section").astype(jnp.int32)
    pairs = []
    for n, slot in enumerate(slots):
        lanes = pl.ds(pl.multiple_of((section ^ slot) * 128, 128), 128)
        pairs.append((w_hbm.at[:, :, lanes, :], outer_ref.at[:, :, n * 128 : (n + 1) * 128, :]))
    return pairs


def second_kernel(x_own_ref, h2_ref, w_hbm, out_ref, outer_ref, acc_ref, sems):
    for copy in start_all(two_slots(w_hbm, outer_ref, (0, 3)), sems):
        copy.wait()
    conv(h2_ref, [outer_ref], acc_ref)
    for i in range(HS):
        rows = slice(i * W, (i + 1) * W)
        out_ref[rows, :] = x_own_ref[rows, :].astype(F32) + gathered(acc_ref, i)


def third_kernel(part_hbm, far_hbm, w_hbm, out_ref, outer_ref, acc_ref, far_ref, part_ref, sems):
    copies = start_all(two_slots(w_hbm, outer_ref, (1, 2)) + [(far_hbm, far_ref), (part_hbm, part_ref)], sems)
    for copy in copies[:3]:
        copy.wait()
    conv(far_ref, [outer_ref], acc_ref)
    copies[3].wait()
    for i in range(HS):
        out_ref[i] = (part_ref[i * W : (i + 1) * W, :] + gathered(acc_ref, i)).astype(BF16)


VM = pl.BlockSpec(memory_space=pltpu.VMEM)
HB = pl.BlockSpec(memory_space=pl.ANY)


def trade(value, across):
    pairs = []
    for row in range(FRAMES):
        for section in range(4):
            y = 4 * (row // 2 % 2) + section
            y = (((y + 1) ^ 1) - 1) % 8 if across else y ^ 1
            there = row // 4 * 4 + y // 4 * 2 + row % 2
            pairs.append((section * FRAMES + row, y % 4 * FRAMES + there))
    return lax.ppermute(value, ("section", "rows"), pairs)


def swap(value):
    return lax.ppermute(value, "rows", [(row, row ^ 1) for row in range(FRAMES)])


def block(latents, w_in, w_time, w_first, w_second):
    packed, half = pl.pallas_call(
        pack_kernel,
        out_shape=[
            jax.ShapeDtypeStruct((FRAMES, 1, MSG), BF16),
            jax.ShapeDtypeStruct((3, 3, 256, 128), BF16),
        ],
        in_specs=[VM, HB],
        out_specs=[VM, VM],
        scratch_shapes=[pltpu.VMEM((MSG, LF), F32), pltpu.SemaphoreType.DMA],
    )(latents.transpose(0, 3, 2, 1).reshape(CLIPS * LOCAL, LATC, LF), w_first)
    cross = trade(half, True)
    recv = lax.all_to_all(packed, "rows", split_axis=0, concat_axis=0, tiled=True)
    cross_swap = swap(cross)
    taps = pl.pallas_call(
        taps_kernel,
        out_shape=jax.ShapeDtypeStruct((MSG, 2 * CH), BF16),
        in_specs=[VM],
        out_specs=VM,
        scratch_shapes=[pltpu.VMEM((16, CH), F32)],
        compiler_params=pltpu.CompilerParams(vmem_limit_bytes=67_000_000),
    )(w_in)
    cell = np.arange(CELLS)[:, None]
    rows_of_cell = jnp.asarray(np.arange(FRAMES)[None] == cell // LOCAL, BF16)
    lanes_of_cell = jnp.asarray(np.arange(MSG)[None] // 16 == cell % LOCAL, F32)
    x_own, h2 = pl.pallas_call(
        first_kernel,
        out_shape=[
            jax.ShapeDtypeStruct((CELLS, 128), BF16),
            jax.ShapeDtypeStruct((CELLS, 256), BF16),
        ],
        in_specs=[VM] * 4 + [HB] * 4,
        out_specs=[VM] * 2,
        scratch_shapes=[
            pltpu.VMEM((3, CH, CH), BF16),
            pltpu.VMEM((2, 3, 3, CH, 128), BF16),
            pltpu.VMEM((CELLS, CH), BF16),
            pltpu.VMEM((2, CELLS, CH), BF16),
            pltpu.VMEM((CELLS, CH), BF16),
            pltpu.VMEM((CELLS, CH), BF16),
            pltpu.VMEM((CELLS, 768), F32),
            pltpu.VMEM((CELLS, 256), BF16),
            pltpu.SemaphoreType.DMA((4,)),
        ],
    )(recv, rows_of_cell, lanes_of_cell, taps, w_time, w_first, cross, cross_swap)
    far = trade(h2, False)
    weights = [
        pltpu.VMEM((3, 3, 256, 128), BF16),
        pltpu.VMEM((CELLS, 384), F32),
        pltpu.SemaphoreType.DMA((2,)),
    ]
    part = pl.pallas_call(
        second_kernel,
        out_shape=jax.ShapeDtypeStruct((CELLS, 128), F32),
        in_specs=[VM, VM, HB],
        out_specs=VM,
        scratch_shapes=weights,
        compiler_params=pltpu.CompilerParams(vmem_limit_bytes=67_000_000),
    )(x_own, h2, w_second)
    out = pl.pallas_call(
        third_kernel,
        out_shape=jax.ShapeDtypeStruct((HS, W, 128), BF16),
        in_specs=[HB] * 3,
        out_specs=VM,
        scratch_shapes=weights[:2]
        + [
            pltpu.VMEM((CELLS, 256), BF16),
            pltpu.VMEM((CELLS, 128), F32),
            pltpu.SemaphoreType.DMA((4,)),
        ],
    )(part, far, w_second)
    return out.reshape(1, HS, W, 128)


def solution(mesh):
    in_specs = (
        P(None, None, None, "rows"),
        P(),
        P(),
        P(None, None, None, "section"),
        P(None, None, None, "section"),
    )
    out_specs = P("rows", None, None, "section")
    return jax.shard_map(block, mesh=mesh, in_specs=in_specs, out_specs=out_specs, check_vma=False)
```

```python
import jax
import jax.numpy as jnp
import numpy as np
from jax import lax
from jax.experimental import pallas as pl
from jax.experimental.pallas import tpu as pltpu
from jax.sharding import PartitionSpec as P


CH = 512
LATC = 4
HS = 4
W = 160
CELLS = HS * W
CLIPS = 4
LF = 8
UPS = 4
FRAMES = 128
GROUP = 16
LOCAL = 5
WINDOW = 4
MSG = 2 * LOCAL * WINDOW * LATC
PEERS = 64
STEP = 128

F32 = jnp.float32
BF16 = jnp.bfloat16


def dot(a, b):
    return jnp.dot(a, b, preferred_element_type=F32)


def iota(shape, dim):
    return lax.broadcasted_iota(jnp.int32, shape, dim)


def onehot(cond):
    return jnp.where(cond, 1.0, 0.0).astype(BF16)


def silu(t):
    return 0.5 * t * (1.0 + jnp.tanh(0.5 * t))


def layouts():
    peer = np.arange(PEERS)[:, None]
    row = np.arange(MSG)
    lane = np.arange(MSG)
    picks = [np.arange(LF)[None] == np.maximum(peer % 16 // 2 - 3 + j, 0) for j in range(WINDOW)]
    same_clip = peer // 16 == row[None] // 20 % CLIPS
    home = (row // 80 * LOCAL + row // LATC % LOCAL)[:, None] == lane[None] // 16
    home = home & (row[:, None] % LATC == lane[None] % LATC)
    places = [home & (lane[None] // LATC % WINDOW == j) for j in range(WINDOW)]
    cell = np.arange(CELLS)[:, None]
    owner = cell // LOCAL
    from_peer = np.arange(PEERS)[None] == owner // 4 * 2 + owner % 2
    in_lanes = lane[None] // 16 == owner // 2 % 2 * LOCAL + cell % LOCAL
    pack = jnp.asarray(np.stack(picks), BF16), jnp.asarray(same_clip, F32), jnp.asarray(np.stack(places), BF16)
    return pack, (jnp.asarray(from_peer, BF16), jnp.asarray(in_lanes, F32))


def pack_kernel(lat_ref, other_ref, pick_ref, same_clip_ref, place_ref, out_ref, flat_ref):
    upper = lax.axis_index("rows") // 2 % 2 == 1
    for n in range(CLIPS * LOCAL):
        mine = lat_ref[n].astype(F32)
        theirs = other_ref[n].astype(F32)
        flat_ref[n * LATC : (n + 1) * LATC, :] = jnp.where(upper, theirs, mine)
        flat_ref[80 + n * LATC : 80 + (n + 1) * LATC, :] = jnp.where(upper, mine, theirs)
    flat = flat_ref[...].astype(BF16)
    total = jnp.zeros((PEERS, MSG), F32)
    for j in range(WINDOW):
        taken = lax.dot_general(pick_ref[j], flat, (((1,), (1,)), ((), ())), preferred_element_type=F32)
        total = total + dot((taken * same_clip_ref[...]).astype(BF16), place_ref[j])
    out_ref[:, 0, :] = total.astype(BF16)


def loop(body, rows=CELLS, step=STEP):
    def wrapped(i, carry):
        return body(pl.ds(pl.multiple_of(i * step, step), step), carry)

    return wrapped, rows // step


def group_total(sums):
    lane = iota(sums.shape, 1)
    width = sums.shape[1]
    for d in (1, 2, 4, 8):
        up = pltpu.roll(sums, d, 1)
        down = pltpu.roll(sums, width - d, 1)
        sums = sums + jnp.where((lane & d) != 0, up, down)
    return sums


def norm_silu(src_ref, dst_ref, width):
    count = float(CELLS * GROUP)

    def add(rows, carry):
        return carry + jnp.sum(src_ref[rows, :].astype(F32).reshape(STEP // 8, 8, width), axis=0)

    def total(fn):
        body, n = loop(fn)
        part = lax.fori_loop(0, n, body, jnp.zeros((8, width), F32))
        part = jnp.sum(part, axis=0, keepdims=True)
        return group_total(jnp.broadcast_to(part, (8, width)))[:1] / count

    mean = total(add)

    def add_sq(rows, carry):
        t = src_ref[rows, :].astype(F32) - mean
        return carry + jnp.sum((t * t).reshape(STEP // 8, 8, width), axis=0)

    scale = lax.rsqrt(total(add_sq) + 1e-06)

    def write(rows, carry):
        t = (src_ref[rows, :].astype(F32) - mean) * scale
        dst_ref[rows, :] = silu(t).astype(BF16)
        return carry

    body, n = loop(write)
    lax.fori_loop(0, n, body, 0)


def conv(h_ref, weights, acc_ref):
    for dy in (1, 0, 2):
        src = slice(W, CELLS) if dy == 2 else slice(0, CELLS - W) if dy == 0 else slice(0, CELLS)
        dst = slice(W, CELLS) if dy == 0 else slice(0, CELLS - W) if dy == 2 else slice(0, CELLS)
        w = jnp.concatenate([ref[dy, dx] for ref in weights for dx in range(3)], axis=1)
        if dy == 1:
            acc_ref[...] = dot(h_ref[src, :], w)
        else:
            acc_ref[dst, :] += dot(h_ref[src, :], w)


def gathered(acc_ref, i, base=0):
    rows = slice(i * W, (i + 1) * W)
    col = iota((W, 128), 0)
    left = jnp.where(col == 0, 0.0, pltpu.roll(acc_ref[rows, base : base + 128], 1, 0))
    right = jnp.where(col == W - 1, 0.0, pltpu.roll(acc_ref[rows, base + 256 : base + 384], W - 1, 0))
    return left + acc_ref[rows, base + 128 : base + 256] + right


def halves(core):
    mine = pl.ds(pl.multiple_of(core * 256, 256), 256)
    other = pl.ds(pl.multiple_of(256 - core * 256, 256), 256)
    return mine, other


def start_all(pairs, sems):
    copies = [pltpu.make_async_copy(src, dst, sems.at[n]) for n, (src, dst) in enumerate(pairs)]
    for copy in copies:
        copy.start()
    return copies


def my_place():
    return lax.axis_index("rows").astype(jnp.int32), lax.axis_index("section").astype(jnp.int32)


def inner_quarters(h_ref, weights, acc_ref, h1_ref, dst_ref):
    conv(h_ref, weights, acc_ref)
    for n in range(len(weights)):
        for i in range(HS):
            h1_ref[i * W : (i + 1) * W, n * 128 : (n + 1) * 128] = gathered(acc_ref, i, n * 384).astype(BF16)
    norm_silu(h1_ref, dst_ref, len(weights) * 128)


def taps_kernel(w_in_ref, out_ref, taps_ref):
    taps_ref[...] = jnp.zeros_like(taps_ref)
    for k in range(3):
        taps_ref[k * LATC : (k + 1) * LATC, :] = w_in_ref[k].astype(F32)
    taps = taps_ref[...].astype(BF16)
    lane = iota((MSG, 16), 0) % 16
    tap = iota((MSG, 16), 1)
    for s in range(2):
        out_ref[:, s * CH : (s + 1) * CH] = dot(onehot(lane == tap + s * LATC), taps).astype(BF16)


def first_kernel(recv_ref, rows_of_cell_ref, lanes_of_cell_ref, taps_ref, w_time_hbm, own_hbm, cross_hbm, cross_swap_hbm, x_own_ref, h2_ref,
                 w_time_ref, inner_ref, u_ref, v_ref, x_ref, h_ref, acc_ref, h1_ref, sems):
    row, section = my_place()
    mine, other = halves(row % 2)
    copies = start_all(
        [
            (w_time_hbm, w_time_ref),
            (own_hbm, inner_ref.at[0]),
            (cross_hbm, inner_ref.at[1, :, :, mine, :]),
            (cross_swap_hbm, inner_ref.at[1, :, :, other, :]),
        ],
        sems,
    )
    spread = (dot(rows_of_cell_ref[...], recv_ref[:, 0, :]) * lanes_of_cell_ref[...]).astype(BF16)
    for s in range(2):
        u = dot(spread, taps_ref[:, s * CH : (s + 1) * CH]).astype(BF16)
        if s == 1:
            u_ref[...] = u
        v_ref[s] = silu(u.astype(F32)).astype(BF16)
    sub = row % UPS
    total = u_ref[...].astype(F32)
    copies[0].wait()
    for k in range(3):
        which = (sub >= 2 - k).astype(jnp.int32)
        total = total + dot(v_ref[which], w_time_ref[k])
    x_ref[...] = total.astype(BF16)
    x_own_ref[...] = x_ref[:, pl.ds(pl.multiple_of(section * 128, 128), 128)]
    norm_silu(x_ref, h_ref, CH)
    for copy in copies[1:]:
        copy.wait()
    inner_quarters(h_ref, [inner_ref.at[0], inner_ref.at[1]], acc_ref, h1_ref, h2_ref)


def two_slots(w_hbm, outer_ref, slots):
    section = lax.axis_index("section").astype(jnp.int32)
    pairs = []
    for n, slot in enumerate(slots):
        lanes = pl.ds(pl.multiple_of((section ^ slot) * 128, 128), 128)
        pairs.append((w_hbm.at[:, :, lanes, :], outer_ref.at[:, :, n * 128 : (n + 1) * 128, :]))
    return pairs


def second_kernel(x_own_ref, h2_ref, w_hbm, out_ref, outer_ref, acc_ref, sems):
    for copy in start_all(two_slots(w_hbm, outer_ref, (0, 3)), sems):
        copy.wait()
    conv(h2_ref, [outer_ref], acc_ref)
    for i in range(HS):
        rows = slice(i * W, (i + 1) * W)
        out_ref[rows, :] = x_own_ref[rows, :].astype(F32) + gathered(acc_ref, i)


def third_kernel(part_hbm, far_hbm, w_hbm, out_ref, outer_ref, acc_ref, far_ref, part_ref, sems):
    copies = start_all(two_slots(w_hbm, outer_ref, (1, 2)) + [(far_hbm, far_ref), (part_hbm, part_ref)], sems)
    for copy in copies[:3]:
        copy.wait()
    conv(far_ref, [outer_ref], acc_ref)
    copies[3].wait()
    for i in range(HS):
        out_ref[i] = (part_ref[i * W : (i + 1) * W, :] + gathered(acc_ref, i)).astype(BF16)


VM = pl.BlockSpec(memory_space=pltpu.VMEM)
HB = pl.BlockSpec(memory_space=pl.ANY)


def trade(value, across):
    pairs = []
    for row in range(FRAMES):
        for section in range(4):
            y = 4 * (row // 2 % 2) + section
            y = (((y + 1) ^ 1) - 1) % 8 if across else y ^ 1
            there = row // 4 * 4 + y // 4 * 2 + row % 2
            pairs.append((section * FRAMES + row, y % 4 * FRAMES + there))
    return lax.ppermute(value, ("section", "rows"), pairs)


def other_y_hi(value):
    pairs = []
    for row in range(FRAMES):
        for section in range(4):
            y = (4 * (row // 2 % 2) + section + (2 if section >= 2 else -2)) % 8
            there = row // 4 * 4 + y // 4 * 2 + row % 2
            pairs.append((section * FRAMES + row, y % 4 * FRAMES + there))
    return lax.ppermute(value, ("section", "rows"), pairs)


def swap(value):
    return lax.ppermute(value, "rows", [(row, row ^ 1) for row in range(FRAMES)])


def block(latents, w_in, w_time, w_first, w_second):
    pack_constants, cell_constants = layouts()
    lat = latents.transpose(0, 3, 2, 1).reshape(CLIPS * LOCAL, LATC, LF)
    lat_other = other_y_hi(lat)
    core = lax.axis_index("rows").astype(jnp.int32) % 2
    half = lax.dynamic_slice_in_dim(w_first, core * 256, 256, 2)
    cross = trade(half, True)
    packed = pl.pallas_call(
        pack_kernel,
        out_shape=jax.ShapeDtypeStruct((PEERS, 1, MSG), BF16),
        in_specs=[VM] * 5,
        out_specs=VM,
        scratch_shapes=[pltpu.VMEM((MSG, LF), F32)],
    )(lat, lat_other, *pack_constants)
    groups = [[row for row in range(FRAMES) if row // 2 % 2 == y_hi] for y_hi in range(2)]
    recv = lax.all_to_all(packed, "rows", split_axis=0, concat_axis=0, axis_index_groups=groups, tiled=True)
    cross_swap = swap(cross)
    taps = pl.pallas_call(
        taps_kernel,
        out_shape=jax.ShapeDtypeStruct((MSG, 2 * CH), BF16),
        in_specs=[VM],
        out_specs=VM,
        scratch_shapes=[pltpu.VMEM((16, CH), F32)],
        compiler_params=pltpu.CompilerParams(vmem_limit_bytes=67_000_000),
    )(w_in)
    x_own, h2 = pl.pallas_call(
        first_kernel,
        out_shape=[
            jax.ShapeDtypeStruct((CELLS, 128), BF16),
            jax.ShapeDtypeStruct((CELLS, 256), BF16),
        ],
        in_specs=[VM] * 4 + [HB] * 4,
        out_specs=[VM] * 2,
        scratch_shapes=[
            pltpu.VMEM((3, CH, CH), BF16),
            pltpu.VMEM((2, 3, 3, CH, 128), BF16),
            pltpu.VMEM((CELLS, CH), BF16),
            pltpu.VMEM((2, CELLS, CH), BF16),
            pltpu.VMEM((CELLS, CH), BF16),
            pltpu.VMEM((CELLS, CH), BF16),
            pltpu.VMEM((CELLS, 768), F32),
            pltpu.VMEM((CELLS, 256), BF16),
            pltpu.SemaphoreType.DMA((4,)),
        ],
    )(recv, *cell_constants, taps, w_time, w_first, cross, cross_swap)
    far = trade(h2, False)
    weights = [
        pltpu.VMEM((3, 3, 256, 128), BF16),
        pltpu.VMEM((CELLS, 384), F32),
        pltpu.SemaphoreType.DMA((2,)),
    ]
    part = pl.pallas_call(
        second_kernel,
        out_shape=jax.ShapeDtypeStruct((CELLS, 128), F32),
        in_specs=[VM, VM, HB],
        out_specs=VM,
        scratch_shapes=weights,
        compiler_params=pltpu.CompilerParams(vmem_limit_bytes=67_000_000),
    )(x_own, h2, w_second)
    out = pl.pallas_call(
        third_kernel,
        out_shape=jax.ShapeDtypeStruct((HS, W, 128), BF16),
        in_specs=[HB] * 3,
        out_specs=VM,
        scratch_shapes=weights[:2]
        + [
            pltpu.VMEM((CELLS, 256), BF16),
            pltpu.VMEM((CELLS, 128), F32),
            pltpu.SemaphoreType.DMA((4,)),
        ],
    )(part, far, w_second)
    return out.reshape(1, HS, W, 128)


def solution(mesh):
    in_specs = (
        P(None, None, None, "rows"),
        P(),
        P(),
        P(None, None, None, "section"),
        P(None, None, None, "section"),
    )
    out_specs = P("rows", None, None, "section")
    return jax.shard_map(block, mesh=mesh, in_specs=in_specs, out_specs=out_specs, check_vma=False)
```

```python
import jax
import jax.numpy as jnp
import numpy as np
from jax import lax
from jax.experimental import pallas as pl
from jax.experimental.pallas import tpu as pltpu
from jax.sharding import PartitionSpec as P


CH = 512
LATC = 4
HS = 4
W = 160
CELLS = HS * W
CLIPS = 4
LF = 8
UPS = 4
FRAMES = 128
GROUP = 16
LOCAL = 5
WINDOW = 4
MSG = 2 * LOCAL * WINDOW * LATC
PEERS = 64
STEP = 128

F32 = jnp.float32
BF16 = jnp.bfloat16


def dot(a, b):
    return jnp.dot(a, b, preferred_element_type=F32)


def iota(shape, dim):
    return lax.broadcasted_iota(jnp.int32, shape, dim)


def onehot(cond):
    return jnp.where(cond, 1.0, 0.0).astype(BF16)


def silu(t):
    return 0.5 * t * (1.0 + jnp.tanh(0.5 * t))


def layouts():
    peer = np.arange(PEERS)[:, None]
    row = np.arange(MSG)
    lane = np.arange(MSG)
    picks = [np.arange(LF)[None] == np.maximum(peer % 16 // 2 - 3 + j, 0) for j in range(WINDOW)]
    same_clip = peer // 16 == row[None] // 20 % CLIPS
    home = (row // 80 * LOCAL + row // LATC % LOCAL)[:, None] == lane[None] // 16
    home = home & (row[:, None] % LATC == lane[None] % LATC)
    places = [home & (lane[None] // LATC % WINDOW == j) for j in range(WINDOW)]
    cell = np.arange(CELLS)[:, None]
    owner = cell // LOCAL
    from_peer = np.arange(PEERS)[None] == owner // 4 * 2 + owner % 2
    in_lanes = lane[None] // 16 == owner // 2 % 2 * LOCAL + cell % LOCAL
    pack = jnp.asarray(np.stack(picks), BF16), jnp.asarray(same_clip, F32), jnp.asarray(np.stack(places), BF16)
    return pack, (jnp.asarray(from_peer, BF16), jnp.asarray(in_lanes, BF16))


def half_kernel(w_ref, half_ref, sem):
    mine, _ = halves(lax.axis_index("rows") % 2)
    cut = pltpu.make_async_copy(w_ref.at[:, :, mine, :], half_ref, sem)
    cut.start()
    cut.wait()


def pack_kernel(lat_ref, other_ref, pick_ref, same_clip_ref, place_ref, out_ref, flat_ref):
    upper = lax.axis_index("rows") // 2 % 2 == 1
    for n in range(CLIPS * LOCAL):
        mine = lat_ref[n].astype(F32)
        theirs = other_ref[n].astype(F32)
        flat_ref[n * LATC : (n + 1) * LATC, :] = jnp.where(upper, theirs, mine)
        flat_ref[80 + n * LATC : 80 + (n + 1) * LATC, :] = jnp.where(upper, mine, theirs)
    flat = flat_ref[...].astype(BF16)
    total = jnp.zeros((PEERS, MSG), F32)
    for j in range(WINDOW):
        taken = lax.dot_general(pick_ref[j], flat, (((1,), (1,)), ((), ())), preferred_element_type=F32)
        total = total + dot((taken * same_clip_ref[...]).astype(BF16), place_ref[j])
    out_ref[:, 0, :] = total.astype(BF16)


def loop(body, rows=CELLS, step=STEP):
    def wrapped(i, carry):
        return body(pl.ds(pl.multiple_of(i * step, step), step), carry)

    return wrapped, rows // step


def group_total(sums):
    lane = iota(sums.shape, 1)
    width = sums.shape[1]
    for d in (1, 2, 4, 8):
        up = pltpu.roll(sums, d, 1)
        down = pltpu.roll(sums, width - d, 1)
        sums = sums + jnp.where((lane & d) != 0, up, down)
    return sums


def norm_silu(src_ref, dst_ref, width):
    count = float(CELLS * GROUP)

    def add(rows, carry):
        return carry + jnp.sum(src_ref[rows, :].astype(F32).reshape(STEP // 8, 8, width), axis=0)

    def total(fn):
        body, n = loop(fn)
        part = lax.fori_loop(0, n, body, jnp.zeros((8, width), F32))
        part = jnp.sum(part, axis=0, keepdims=True)
        return group_total(jnp.broadcast_to(part, (8, width)))[:1] / count

    mean = total(add)

    def add_sq(rows, carry):
        t = src_ref[rows, :].astype(F32) - mean
        return carry + jnp.sum((t * t).reshape(STEP // 8, 8, width), axis=0)

    scale = lax.rsqrt(total(add_sq) + 1e-06)

    def write(rows, carry):
        t = (src_ref[rows, :].astype(F32) - mean) * scale
        dst_ref[rows, :] = silu(t).astype(BF16)
        return carry

    body, n = loop(write)
    lax.fori_loop(0, n, body, 0)


def conv(h_ref, weights, acc_ref):
    for dy in (1, 0, 2):
        src = slice(W, CELLS) if dy == 2 else slice(0, CELLS - W) if dy == 0 else slice(0, CELLS)
        dst = slice(W, CELLS) if dy == 0 else slice(0, CELLS - W) if dy == 2 else slice(0, CELLS)
        w = jnp.concatenate([ref[dy, dx] for ref in weights for dx in range(3)], axis=1)
        if dy == 1:
            acc_ref[...] = dot(h_ref[src, :], w)
        else:
            acc_ref[dst, :] += dot(h_ref[src, :], w)


def gathered(acc_ref, i, base=0):
    rows = slice(i * W, (i + 1) * W)
    col = iota((W, 128), 0)
    left = jnp.where(col == 0, 0.0, pltpu.roll(acc_ref[rows, base : base + 128], 1, 0))
    right = jnp.where(col == W - 1, 0.0, pltpu.roll(acc_ref[rows, base + 256 : base + 384], W - 1, 0))
    return left + acc_ref[rows, base + 128 : base + 256] + right


def halves(core):
    mine = pl.ds(pl.multiple_of(core * 256, 256), 256)
    other = pl.ds(pl.multiple_of(256 - core * 256, 256), 256)
    return mine, other


def start_all(pairs, sems):
    copies = [pltpu.make_async_copy(src, dst, sems.at[n]) for n, (src, dst) in enumerate(pairs)]
    for copy in copies:
        copy.start()
    return copies


def my_place():
    return lax.axis_index("rows").astype(jnp.int32), lax.axis_index("section").astype(jnp.int32)


def inner_quarters(h_ref, weights, acc_ref, h1_ref, dst_ref):
    conv(h_ref, weights, acc_ref)
    for n in range(len(weights)):
        for i in range(HS):
            h1_ref[i * W : (i + 1) * W, n * 128 : (n + 1) * 128] = gathered(acc_ref, i, n * 384).astype(BF16)
    norm_silu(h1_ref, dst_ref, len(weights) * 128)


def taps_kernel(w_in_ref, out_ref, taps_ref):
    taps_ref[...] = jnp.zeros_like(taps_ref)
    for k in range(3):
        taps_ref[k * LATC : (k + 1) * LATC, :] = w_in_ref[k].astype(F32)
    taps = taps_ref[...].astype(BF16)
    lane = iota((MSG, 16), 0) % 16
    tap = iota((MSG, 16), 1)
    for s in range(2):
        out_ref[:, s * CH : (s + 1) * CH] = dot(onehot(lane == tap + s * LATC), taps).astype(BF16)


def first_kernel(recv_hbm, from_peer_hbm, in_lanes_hbm, taps_hbm, w_time_hbm, own_hbm, cross_hbm, cross_swap_hbm,
                 x_own_ref, h2_ref,
                 recv_ref, from_peer_ref, in_lanes_ref, taps_ref, w_time_ref, inner_ref, u_ref, v_ref, x_ref, h_ref,
                 acc_ref, h1_ref, sems):
    row, section = my_place()
    mine, other = halves(row % 2)
    copies = start_all(
        [
            (recv_hbm, recv_ref),
            (from_peer_hbm, from_peer_ref),
            (in_lanes_hbm, in_lanes_ref),
            (taps_hbm, taps_ref),
            (w_time_hbm, w_time_ref),
            (own_hbm, inner_ref.at[0]),
            (cross_hbm, inner_ref.at[1, :, :, mine, :]),
            (cross_swap_hbm, inner_ref.at[1, :, :, other, :]),
        ],
        sems,
    )
    for copy in copies[:4]:
        copy.wait()
    sub = row % UPS
    spread = (dot(from_peer_ref[...], recv_ref[:, 0, :]) * in_lanes_ref[...].astype(F32)).astype(BF16)
    u_before = dot(spread, taps_ref[:, :CH]).astype(BF16)
    before = silu(u_before.astype(F32)).astype(BF16)
    u_ref[...] = dot(spread, taps_ref[:, CH:]).astype(BF16)
    now = silu(u_ref[...].astype(F32)).astype(BF16)
    v_ref[:, :CH] = jnp.where(sub >= 2, now, before)
    v_ref[:, CH : 2 * CH] = jnp.where(sub >= 1, now, before)
    v_ref[:, 2 * CH :] = now
    copies[4].wait()
    total = u_ref[...].astype(F32) + dot(v_ref[...], w_time_ref[...].reshape(3 * CH, CH))
    x_ref[...] = total.astype(BF16)
    x_own_ref[...] = x_ref[:, pl.ds(pl.multiple_of(section * 128, 128), 128)]
    norm_silu(x_ref, h_ref, CH)
    for copy in copies[5:]:
        copy.wait()
    inner_quarters(h_ref, [inner_ref.at[0], inner_ref.at[1]], acc_ref, h1_ref, h2_ref)


def two_slots(w_hbm, outer_ref, slots):
    section = lax.axis_index("section").astype(jnp.int32)
    pairs = []
    for n, slot in enumerate(slots):
        lanes = pl.ds(pl.multiple_of((section ^ slot) * 128, 128), 128)
        pairs.append((w_hbm.at[:, :, lanes, :], outer_ref.at[:, :, n * 128 : (n + 1) * 128, :]))
    return pairs


def second_kernel(x_own_ref, h2_ref, w_hbm, out_ref, outer_ref, acc_ref, sems):
    for copy in start_all(two_slots(w_hbm, outer_ref, (0, 3)), sems):
        copy.wait()
    conv(h2_ref, [outer_ref], acc_ref)
    for i in range(HS):
        rows = slice(i * W, (i + 1) * W)
        out_ref[rows, :] = x_own_ref[rows, :].astype(F32) + gathered(acc_ref, i)


def third_kernel(part_hbm, far_hbm, w_hbm, out_ref, outer_ref, acc_ref, far_ref, part_ref, sems):
    copies = start_all(two_slots(w_hbm, outer_ref, (1, 2)) + [(far_hbm, far_ref), (part_hbm, part_ref)], sems)
    for copy in copies[:3]:
        copy.wait()
    conv(far_ref, [outer_ref], acc_ref)
    copies[3].wait()
    for i in range(HS):
        out_ref[i] = (part_ref[i * W : (i + 1) * W, :] + gathered(acc_ref, i)).astype(BF16)


VM = pl.BlockSpec(memory_space=pltpu.VMEM)
HB = pl.BlockSpec(memory_space=pl.ANY)


def trade(value, across):
    pairs = []
    for row in range(FRAMES):
        for section in range(4):
            y = 4 * (row // 2 % 2) + section
            y = (((y + 1) ^ 1) - 1) % 8 if across else y ^ 1
            there = row // 4 * 4 + y // 4 * 2 + row % 2
            pairs.append((section * FRAMES + row, y % 4 * FRAMES + there))
    return lax.ppermute(value, ("section", "rows"), pairs)


def other_y_hi(value):
    pairs = []
    for row in range(FRAMES):
        for section in range(4):
            y = (4 * (row // 2 % 2) + section + (2 if section >= 2 else -2)) % 8
            there = row // 4 * 4 + y // 4 * 2 + row % 2
            pairs.append((section * FRAMES + row, y % 4 * FRAMES + there))
    return lax.ppermute(value, ("section", "rows"), pairs)


def swap(value):
    return lax.ppermute(value, "rows", [(row, row ^ 1) for row in range(FRAMES)])


def block(latents, w_in, w_time, w_first, w_second):
    pack_constants, cell_constants = layouts()
    lat = latents.transpose(0, 3, 2, 1).reshape(CLIPS * LOCAL, LATC, LF)
    lat_other = other_y_hi(lat)
    half = pl.pallas_call(
        half_kernel,
        out_shape=jax.ShapeDtypeStruct((3, 3, 256, 128), BF16),
        in_specs=[HB],
        out_specs=VM,
        scratch_shapes=[pltpu.SemaphoreType.DMA],
        compiler_params=pltpu.CompilerParams(vmem_limit_bytes=67_100_000),
    )(w_first)
    cross = trade(half, True)
    packed = pl.pallas_call(
        pack_kernel,
        out_shape=jax.ShapeDtypeStruct((PEERS, 1, MSG), BF16),
        in_specs=[VM] * 5,
        out_specs=VM,
        scratch_shapes=[pltpu.VMEM((MSG, LF), F32)],
    )(lat, lat_other, *pack_constants)
    groups = [[row for row in range(FRAMES) if row // 2 % 2 == y_hi] for y_hi in range(2)]
    recv = lax.all_to_all(packed, "rows", split_axis=0, concat_axis=0, axis_index_groups=groups, tiled=True)
    cross_swap = swap(cross)
    taps = pl.pallas_call(
        taps_kernel,
        out_shape=jax.ShapeDtypeStruct((MSG, 2 * CH), BF16),
        in_specs=[VM],
        out_specs=VM,
        scratch_shapes=[pltpu.VMEM((16, CH), F32)],
        compiler_params=pltpu.CompilerParams(vmem_limit_bytes=67_000_000),
    )(w_in)
    x_own, h2 = pl.pallas_call(
        first_kernel,
        out_shape=[
            jax.ShapeDtypeStruct((CELLS, 128), BF16),
            jax.ShapeDtypeStruct((CELLS, 256), BF16),
        ],
        in_specs=[HB] * 8,
        out_specs=[VM] * 2,
        scratch_shapes=[
            pltpu.VMEM((PEERS, 1, MSG), BF16),
            pltpu.VMEM((CELLS, PEERS), BF16),
            pltpu.VMEM((CELLS, MSG), BF16),
            pltpu.VMEM((MSG, 2 * CH), BF16),
            pltpu.VMEM((3, CH, CH), BF16),
            pltpu.VMEM((2, 3, 3, CH, 128), BF16),
            pltpu.VMEM((CELLS, CH), BF16),
            pltpu.VMEM((CELLS, 3 * CH), BF16),
            pltpu.VMEM((CELLS, CH), BF16),
            pltpu.VMEM((CELLS, CH), BF16),
            pltpu.VMEM((CELLS, 768), F32),
            pltpu.VMEM((CELLS, 256), BF16),
            pltpu.SemaphoreType.DMA((8,)),
        ],
    )(recv, *cell_constants, taps, w_time, w_first, cross, cross_swap)
    far = trade(h2, False)
    weights = [
        pltpu.VMEM((3, 3, 256, 128), BF16),
        pltpu.VMEM((CELLS, 384), F32),
        pltpu.SemaphoreType.DMA((2,)),
    ]
    part = pl.pallas_call(
        second_kernel,
        out_shape=jax.ShapeDtypeStruct((CELLS, 128), F32),
        in_specs=[VM, VM, HB],
        out_specs=VM,
        scratch_shapes=weights,
        compiler_params=pltpu.CompilerParams(vmem_limit_bytes=67_000_000),
    )(x_own, h2, w_second)
    out = pl.pallas_call(
        third_kernel,
        out_shape=jax.ShapeDtypeStruct((HS, W, 128), BF16),
        in_specs=[HB] * 3,
        out_specs=VM,
        scratch_shapes=weights[:2]
        + [
            pltpu.VMEM((CELLS, 256), BF16),
            pltpu.VMEM((CELLS, 128), F32),
            pltpu.SemaphoreType.DMA((4,)),
        ],
    )(part, far, w_second)
    return out.reshape(1, HS, W, 128)


def solution(mesh):
    in_specs = (
        P(None, None, None, "rows"),
        P(),
        P(),
        P(None, None, None, "section"),
        P(None, None, None, "section"),
    )
    out_specs = P("rows", None, None, "section")
    return jax.shard_map(block, mesh=mesh, in_specs=in_specs, out_specs=out_specs, check_vma=False)
```

```python
import jax
import jax.numpy as jnp
import numpy as np
from jax import lax
from jax.experimental import pallas as pl
from jax.experimental.pallas import tpu as pltpu
from jax.sharding import PartitionSpec as P


CH = 512
LATC = 4
HS = 4
W = 160
CELLS = HS * W
CLIPS = 4
LF = 8
UPS = 4
FRAMES = 128
GROUP = 16
LOCAL = 5
WINDOW = 4
MSG = 2 * LOCAL * WINDOW * LATC
PEERS = 64
STEP = 128

F32 = jnp.float32
BF16 = jnp.bfloat16


def dot(a, b):
    return jnp.dot(a, b, preferred_element_type=F32)


def iota(shape, dim):
    return lax.broadcasted_iota(jnp.int32, shape, dim)


def onehot(cond):
    return jnp.where(cond, 1.0, 0.0).astype(BF16)


def silu(t):
    return 0.5 * t * (1.0 + jnp.tanh(0.5 * t))


def layouts():
    peer = np.arange(PEERS)[:, None]
    row = np.arange(MSG)
    lane = np.arange(MSG)
    picks = [np.arange(LF)[None] == np.maximum(peer % 16 // 2 - 3 + j, 0) for j in range(WINDOW)]
    same_clip = peer // 16 == row[None] // 20 % CLIPS
    home = (row // 80 * LOCAL + row // LATC % LOCAL)[:, None] == lane[None] // 16
    home = home & (row[:, None] % LATC == lane[None] % LATC)
    places = [home & (lane[None] // LATC % WINDOW == j) for j in range(WINDOW)]
    cell = np.arange(CELLS)[:, None]
    owner = cell // LOCAL
    from_peer = np.arange(PEERS)[None] == owner // 4 * 2 + owner % 2
    in_lanes = lane[None] // 16 == owner // 2 % 2 * LOCAL + cell % LOCAL
    pack = jnp.asarray(np.stack(picks), BF16), jnp.asarray(same_clip, F32), jnp.asarray(np.stack(places), BF16)
    return pack, (jnp.asarray(from_peer, BF16), jnp.asarray(in_lanes, BF16))


def pack_kernel(lat_ref, other_ref, pick_ref, same_clip_ref, place_ref, out_ref, flat_ref):
    upper = lax.axis_index("rows") // 2 % 2 == 1
    for n in range(CLIPS * LOCAL):
        mine = lat_ref[n].astype(F32)
        theirs = other_ref[n].astype(F32)
        flat_ref[n * LATC : (n + 1) * LATC, :] = jnp.where(upper, theirs, mine)
        flat_ref[80 + n * LATC : 80 + (n + 1) * LATC, :] = jnp.where(upper, mine, theirs)
    flat = flat_ref[...].astype(BF16)
    total = jnp.zeros((PEERS, MSG), F32)
    for j in range(WINDOW):
        taken = lax.dot_general(pick_ref[j], flat, (((1,), (1,)), ((), ())), preferred_element_type=F32)
        total = total + dot((taken * same_clip_ref[...]).astype(BF16), place_ref[j])
    out_ref[:, 0, :] = total.astype(BF16)


def group_total(sums):
    lane = iota(sums.shape, 1)
    width = sums.shape[1]
    for d in (1, 2, 4, 8):
        up = pltpu.roll(sums, d, 1)
        down = pltpu.roll(sums, width - d, 1)
        sums = sums + jnp.where((lane & d) != 0, up, down)
    return sums


def norm_silu(src_ref, dst_ref, width):
    count = float(CELLS * GROUP)

    def tree(t):
        t = t.reshape(-1, 8, width)
        while t.shape[0] > 1:
            t = t[: t.shape[0] // 2] + t[t.shape[0] // 2 :]
        return t[0]

    def total(part):
        part = jnp.sum(part, axis=0, keepdims=True)
        return group_total(jnp.broadcast_to(part, (8, width)))[:1] / count

    part = jnp.zeros((8, width), F32)
    for r in range(0, CELLS, STEP):
        part = part + tree(src_ref[r : r + STEP, :].astype(F32))
    mean = total(part)
    part = jnp.zeros((8, width), F32)
    for r in range(0, CELLS, STEP):
        t = src_ref[r : r + STEP, :].astype(F32) - mean
        part = part + tree(t * t)
    scale = lax.rsqrt(total(part) + 1e-06)
    for r in range(0, CELLS, STEP):
        t = (src_ref[r : r + STEP, :].astype(F32) - mean) * scale
        dst_ref[r : r + STEP, :] = silu(t).astype(BF16)


def conv(h_ref, weights, acc_ref):
    for dy in (1, 0, 2):
        src = slice(W, CELLS) if dy == 2 else slice(0, CELLS - W) if dy == 0 else slice(0, CELLS)
        dst = slice(W, CELLS) if dy == 0 else slice(0, CELLS - W) if dy == 2 else slice(0, CELLS)
        w = jnp.concatenate([ref[dy, dx] for ref in weights for dx in range(3)], axis=1)
        if dy == 1:
            acc_ref[...] = dot(h_ref[src, :], w)
        else:
            acc_ref[dst, :] += dot(h_ref[src, :], w)


def gathered(acc_ref, i, base=0):
    rows = slice(i * W, (i + 1) * W)
    col = iota((W, 128), 0)
    left = jnp.where(col == 0, 0.0, pltpu.roll(acc_ref[rows, base : base + 128], 1, 0))
    right = jnp.where(col == W - 1, 0.0, pltpu.roll(acc_ref[rows, base + 256 : base + 384], W - 1, 0))
    return left + acc_ref[rows, base + 128 : base + 256] + right


def halves(core):
    mine = pl.ds(pl.multiple_of(core * 256, 256), 256)
    other = pl.ds(pl.multiple_of(256 - core * 256, 256), 256)
    return mine, other


def start_all(pairs, sems):
    copies = [pltpu.make_async_copy(src, dst, sems.at[n]) for n, (src, dst) in enumerate(pairs)]
    for copy in copies:
        copy.start()
    return copies


def my_place():
    return lax.axis_index("rows").astype(jnp.int32), lax.axis_index("section").astype(jnp.int32)


def inner_quarters(h_ref, weights, acc_ref, h1_ref, dst_ref):
    conv(h_ref, weights, acc_ref)
    for n in range(len(weights)):
        for i in range(HS):
            h1_ref[i * W : (i + 1) * W, n * 128 : (n + 1) * 128] = gathered(acc_ref, i, n * 384).astype(BF16)
    norm_silu(h1_ref, dst_ref, len(weights) * 128)


def taps_kernel(w_in_ref, out_ref, taps_ref):
    taps_ref[...] = jnp.zeros_like(taps_ref)
    for k in range(3):
        taps_ref[k * LATC : (k + 1) * LATC, :] = w_in_ref[k].astype(F32)
    taps = taps_ref[...].astype(BF16)
    lane = iota((MSG, 16), 0) % 16
    tap = iota((MSG, 16), 1)
    for s in range(2):
        out_ref[:, s * CH : (s + 1) * CH] = dot(onehot(lane == tap + s * LATC), taps).astype(BF16)


def first_kernel(recv_hbm, from_peer_hbm, in_lanes_hbm, taps_hbm, w_time_hbm, own_hbm, cross_hbm, cross_swap_hbm,
                 x_own_ref, h2_ref,
                 recv_ref, from_peer_ref, in_lanes_ref, taps_ref, w_time_ref, inner_ref, u_ref, v_ref, x_ref, h_ref,
                 acc_ref, h1_ref, sems):
    row, section = my_place()
    mine, other = halves(row % 2)
    copies = start_all(
        [
            (recv_hbm, recv_ref),
            (from_peer_hbm, from_peer_ref),
            (in_lanes_hbm, in_lanes_ref),
            (taps_hbm, taps_ref),
            (w_time_hbm, w_time_ref),
            (own_hbm, inner_ref.at[0]),
            (cross_hbm, inner_ref.at[1, :, :, mine, :]),
            (cross_swap_hbm, inner_ref.at[1, :, :, other, :]),
        ],
        sems,
    )
    for copy in copies[:4]:
        copy.wait()
    sub = row % UPS
    spread = (dot(from_peer_ref[...], recv_ref[:, 0, :]) * in_lanes_ref[...].astype(F32)).astype(BF16)
    u_before = dot(spread, taps_ref[:, :CH]).astype(BF16)
    before = silu(u_before.astype(F32)).astype(BF16)
    u_ref[...] = dot(spread, taps_ref[:, CH:]).astype(BF16)
    now = silu(u_ref[...].astype(F32)).astype(BF16)
    v_ref[:, :CH] = jnp.where(sub >= 2, now, before)
    v_ref[:, CH : 2 * CH] = jnp.where(sub >= 1, now, before)
    v_ref[:, 2 * CH :] = now
    copies[4].wait()
    total = u_ref[...].astype(F32) + dot(v_ref[...], w_time_ref[...].reshape(3 * CH, CH))
    x_ref[...] = total.astype(BF16)
    x_own_ref[...] = x_ref[:, pl.ds(pl.multiple_of(section * 128, 128), 128)]
    norm_silu(x_ref, h_ref, CH)
    for copy in copies[5:]:
        copy.wait()
    inner_quarters(h_ref, [inner_ref.at[0], inner_ref.at[1]], acc_ref, h1_ref, h2_ref)


def two_slots(w_hbm, outer_ref, slots):
    section = lax.axis_index("section").astype(jnp.int32)
    pairs = []
    for n, slot in enumerate(slots):
        lanes = pl.ds(pl.multiple_of((section ^ slot) * 128, 128), 128)
        pairs.append((w_hbm.at[:, :, lanes, :], outer_ref.at[:, :, n * 128 : (n + 1) * 128, :]))
    return pairs


def second_kernel(x_own_ref, h2_ref, w_hbm, out_ref, outer_ref, acc_ref, sems):
    for copy in start_all(two_slots(w_hbm, outer_ref, (0, 3)), sems):
        copy.wait()
    conv(h2_ref, [outer_ref], acc_ref)
    for i in range(HS):
        rows = slice(i * W, (i + 1) * W)
        out_ref[rows, :] = x_own_ref[rows, :].astype(F32) + gathered(acc_ref, i)


def third_kernel(part_hbm, far_hbm, w_hbm, out_ref, outer_ref, acc_ref, far_ref, part_ref, sems):
    copies = start_all(two_slots(w_hbm, outer_ref, (1, 2)) + [(far_hbm, far_ref), (part_hbm, part_ref)], sems)
    for copy in copies[:3]:
        copy.wait()
    conv(far_ref, [outer_ref], acc_ref)
    copies[3].wait()
    for i in range(HS):
        out_ref[i] = (part_ref[i * W : (i + 1) * W, :] + gathered(acc_ref, i)).astype(BF16)


VM = pl.BlockSpec(memory_space=pltpu.VMEM)
HB = pl.BlockSpec(memory_space=pl.ANY)


def trade(value, across):
    pairs = []
    for row in range(FRAMES):
        for section in range(4):
            y = 4 * (row // 2 % 2) + section
            y = (((y + 1) ^ 1) - 1) % 8 if across else y ^ 1
            there = row // 4 * 4 + y // 4 * 2 + row % 2
            pairs.append((section * FRAMES + row, y % 4 * FRAMES + there))
    return lax.ppermute(value, ("section", "rows"), pairs)


def other_y_hi(value):
    pairs = []
    for row in range(FRAMES):
        for section in range(4):
            y = (4 * (row // 2 % 2) + section + (2 if section >= 2 else -2)) % 8
            there = row // 4 * 4 + y // 4 * 2 + row % 2
            pairs.append((section * FRAMES + row, y % 4 * FRAMES + there))
    return lax.ppermute(value, ("section", "rows"), pairs)


def swap(value):
    return lax.ppermute(value, "rows", [(row, row ^ 1) for row in range(FRAMES)])


def block(latents, w_in, w_time, w_first, w_second):
    pack_constants, cell_constants = layouts()
    lat = latents.transpose(0, 3, 2, 1).reshape(CLIPS * LOCAL, LATC, LF)
    lat_other = other_y_hi(lat)
    core = lax.axis_index("rows").astype(jnp.int32) % 2
    half = lax.dynamic_slice_in_dim(w_first, core * 256, 256, 2)
    cross = trade(half, True)
    packed = pl.pallas_call(
        pack_kernel,
        out_shape=jax.ShapeDtypeStruct((PEERS, 1, MSG), BF16),
        in_specs=[VM] * 5,
        out_specs=VM,
        scratch_shapes=[pltpu.VMEM((MSG, LF), F32)],
    )(lat, lat_other, *pack_constants)
    groups = [[row for row in range(FRAMES) if row // 2 % 2 == y_hi] for y_hi in range(2)]
    recv = lax.all_to_all(packed, "rows", split_axis=0, concat_axis=0, axis_index_groups=groups, tiled=True)
    cross_swap = swap(cross)
    taps = pl.pallas_call(
        taps_kernel,
        out_shape=jax.ShapeDtypeStruct((MSG, 2 * CH), BF16),
        in_specs=[VM],
        out_specs=VM,
        scratch_shapes=[pltpu.VMEM((16, CH), F32)],
        compiler_params=pltpu.CompilerParams(vmem_limit_bytes=67_000_000),
    )(w_in)
    x_own, h2 = pl.pallas_call(
        first_kernel,
        out_shape=[
            jax.ShapeDtypeStruct((CELLS, 128), BF16),
            jax.ShapeDtypeStruct((CELLS, 256), BF16),
        ],
        in_specs=[HB] * 8,
        out_specs=[VM] * 2,
        scratch_shapes=[
            pltpu.VMEM((PEERS, 1, MSG), BF16),
            pltpu.VMEM((CELLS, PEERS), BF16),
            pltpu.VMEM((CELLS, MSG), BF16),
            pltpu.VMEM((MSG, 2 * CH), BF16),
            pltpu.VMEM((3, CH, CH), BF16),
            pltpu.VMEM((2, 3, 3, CH, 128), BF16),
            pltpu.VMEM((CELLS, CH), BF16),
            pltpu.VMEM((CELLS, 3 * CH), BF16),
            pltpu.VMEM((CELLS, CH), BF16),
            pltpu.VMEM((CELLS, CH), BF16),
            pltpu.VMEM((CELLS, 768), F32),
            pltpu.VMEM((CELLS, 256), BF16),
            pltpu.SemaphoreType.DMA((8,)),
        ],
    )(recv, *cell_constants, taps, w_time, w_first, cross, cross_swap)
    far = trade(h2, False)
    weights = [
        pltpu.VMEM((3, 3, 256, 128), BF16),
        pltpu.VMEM((CELLS, 384), F32),
        pltpu.SemaphoreType.DMA((2,)),
    ]
    part = pl.pallas_call(
        second_kernel,
        out_shape=jax.ShapeDtypeStruct((CELLS, 128), F32),
        in_specs=[VM, VM, HB],
        out_specs=VM,
        scratch_shapes=weights,
        compiler_params=pltpu.CompilerParams(vmem_limit_bytes=67_000_000),
    )(x_own, h2, w_second)
    out = pl.pallas_call(
        third_kernel,
        out_shape=jax.ShapeDtypeStruct((HS, W, 128), BF16),
        in_specs=[HB] * 3,
        out_specs=VM,
        scratch_shapes=weights[:2]
        + [
            pltpu.VMEM((CELLS, 256), BF16),
            pltpu.VMEM((CELLS, 128), F32),
            pltpu.SemaphoreType.DMA((4,)),
        ],
    )(part, far, w_second)
    return out.reshape(1, HS, W, 128)


def solution(mesh):
    in_specs = (
        P(None, None, None, "rows"),
        P(),
        P(),
        P(None, None, None, "section"),
        P(None, None, None, "section"),
    )
    out_specs = P("rows", None, None, "section")
    return jax.shard_map(block, mesh=mesh, in_specs=in_specs, out_specs=out_specs, check_vma=False)
```

```python
import jax
import jax.numpy as jnp
import numpy as np
from jax import lax
from jax.experimental import pallas as pl
from jax.experimental.pallas import tpu as pltpu
from jax.sharding import PartitionSpec as P


CH = 512
LATC = 4
HS = 4
W = 160
CELLS = HS * W
CLIPS = 4
LF = 8
UPS = 4
FRAMES = 128
GROUP = 16
LOCAL = 5
WINDOW = 4
MSG = 2 * LOCAL * WINDOW * LATC
PEERS = 64
STEP = 128

F32 = jnp.float32
BF16 = jnp.bfloat16


def dot(a, b):
    return jnp.dot(a, b, preferred_element_type=F32)


def iota(shape, dim):
    return lax.broadcasted_iota(jnp.int32, shape, dim)


def onehot(cond):
    return jnp.where(cond, 1.0, 0.0).astype(BF16)


def silu(t):
    return 0.5 * t * (1.0 + jnp.tanh(0.5 * t))


def layouts():
    peer = np.arange(PEERS)[:, None]
    row = np.arange(MSG)
    lane = np.arange(MSG)
    picks = [np.arange(LF)[None] == np.maximum(peer % 16 // 2 - 3 + j, 0) for j in range(WINDOW)]
    same_clip = peer // 16 == row[None] // 20 % CLIPS
    home = (row // 80 * LOCAL + row // LATC % LOCAL)[:, None] == lane[None] // 16
    home = home & (row[:, None] % LATC == lane[None] % LATC)
    places = [home & (lane[None] // LATC % WINDOW == j) for j in range(WINDOW)]
    cell = np.arange(CELLS)[:, None]
    owner = cell // LOCAL
    from_peer = np.arange(PEERS)[None] == owner // 4 * 2 + owner % 2
    in_lanes = lane[None] // 16 == owner // 2 % 2 * LOCAL + cell % LOCAL
    pack = jnp.asarray(np.stack(picks), BF16), jnp.asarray(same_clip, F32), jnp.asarray(np.stack(places), BF16)
    return pack, (jnp.asarray(from_peer, BF16), jnp.asarray(in_lanes, BF16))


def pack_kernel(lat_ref, other_ref, pick_ref, same_clip_ref, place_ref, out_ref, flat_ref):
    upper = lax.axis_index("rows") // 2 % 2 == 1
    for n in range(CLIPS * LOCAL):
        mine = lat_ref[n].astype(F32)
        theirs = other_ref[n].astype(F32)
        flat_ref[n * LATC : (n + 1) * LATC, :] = jnp.where(upper, theirs, mine)
        flat_ref[80 + n * LATC : 80 + (n + 1) * LATC, :] = jnp.where(upper, mine, theirs)
    flat = flat_ref[...].astype(BF16)
    total = jnp.zeros((PEERS, MSG), F32)
    for j in range(WINDOW):
        taken = lax.dot_general(pick_ref[j], flat, (((1,), (1,)), ((), ())), preferred_element_type=F32)
        total = total + dot((taken * same_clip_ref[...]).astype(BF16), place_ref[j])
    out_ref[:, 0, :] = total.astype(BF16)


def group_total(sums):
    lane = iota(sums.shape, 1)
    width = sums.shape[1]
    for d in (1, 2, 4, 8):
        up = pltpu.roll(sums, d, 1)
        down = pltpu.roll(sums, width - d, 1)
        sums = sums + jnp.where((lane & d) != 0, up, down)
    return sums


def norm_silu(src_ref, dst_ref, width):
    count = float(CELLS * GROUP)

    def tree(t):
        t = t.reshape(-1, 8, width)
        while t.shape[0] > 1:
            t = t[: t.shape[0] // 2] + t[t.shape[0] // 2 :]
        return t[0]

    def total(part):
        part = jnp.sum(part, axis=0, keepdims=True)
        return group_total(jnp.broadcast_to(part, (8, width)))[:1] / count

    part = jnp.zeros((8, width), F32)
    for r in range(0, CELLS, STEP):
        part = part + tree(src_ref[r : r + STEP, :].astype(F32))
    mean = total(part)
    part = jnp.zeros((8, width), F32)
    for r in range(0, CELLS, STEP):
        t = src_ref[r : r + STEP, :].astype(F32) - mean
        part = part + tree(t * t)
    scale = lax.rsqrt(total(part) + 1e-06)
    for r in range(0, CELLS, STEP):
        t = (src_ref[r : r + STEP, :].astype(F32) - mean) * scale
        dst_ref[r : r + STEP, :] = silu(t).astype(BF16)


def conv(h_ref, weights, acc_ref):
    for dy in (1, 0, 2):
        src = slice(W, CELLS) if dy == 2 else slice(0, CELLS - W) if dy == 0 else slice(0, CELLS)
        dst = slice(W, CELLS) if dy == 0 else slice(0, CELLS - W) if dy == 2 else slice(0, CELLS)
        w = jnp.concatenate([ref[dy, dx] for ref in weights for dx in range(3)], axis=1)
        if dy == 1:
            acc_ref[...] = dot(h_ref[src, :], w)
        else:
            acc_ref[dst, :] += dot(h_ref[src, :], w)


def gathered(acc_ref, i, base=0):
    rows = slice(i * W, (i + 1) * W)
    col = iota((W, 128), 0)
    left = jnp.where(col == 0, 0.0, pltpu.roll(acc_ref[rows, base : base + 128], 1, 0))
    right = jnp.where(col == W - 1, 0.0, pltpu.roll(acc_ref[rows, base + 256 : base + 384], W - 1, 0))
    return left + acc_ref[rows, base + 128 : base + 256] + right


def halves(core):
    mine = pl.ds(pl.multiple_of(core * 256, 256), 256)
    other = pl.ds(pl.multiple_of(256 - core * 256, 256), 256)
    return mine, other


def start_all(pairs, sems):
    copies = [pltpu.make_async_copy(src, dst, sems.at[n]) for n, (src, dst) in enumerate(pairs)]
    for copy in copies:
        copy.start()
    return copies


def my_place():
    return lax.axis_index("rows").astype(jnp.int32), lax.axis_index("section").astype(jnp.int32)


def inner_quarters(h_ref, weights, acc_ref, h1_ref, dst_ref):
    conv(h_ref, weights, acc_ref)
    for n in range(len(weights)):
        for i in range(HS):
            h1_ref[i * W : (i + 1) * W, n * 128 : (n + 1) * 128] = gathered(acc_ref, i, n * 384).astype(BF16)
    norm_silu(h1_ref, dst_ref, len(weights) * 128)


def taps_kernel(w_in_ref, out_ref, taps_ref):
    taps_ref[...] = jnp.zeros_like(taps_ref)
    for k in range(3):
        taps_ref[k * LATC : (k + 1) * LATC, :] = w_in_ref[k].astype(F32)
    taps = taps_ref[...].astype(BF16)
    lane = iota((MSG, 16), 0) % 16
    tap = iota((MSG, 16), 1)
    for s in range(2):
        out_ref[:, s * CH : (s + 1) * CH] = dot(onehot(lane == tap + s * LATC), taps).astype(BF16)


def first_kernel(recv_hbm, from_peer_hbm, in_lanes_hbm, taps_hbm, w_time_hbm, own_hbm, x_own_ref, h_ref, h2_ref,
                 recv_ref, from_peer_ref, in_lanes_ref, taps_ref, w_time_ref, inner_ref, u_ref, v_ref, x_ref,
                 acc_ref, h1_ref, sems):
    row, section = my_place()
    copies = start_all(
        [
            (recv_hbm, recv_ref),
            (from_peer_hbm, from_peer_ref),
            (in_lanes_hbm, in_lanes_ref),
            (taps_hbm, taps_ref),
            (w_time_hbm, w_time_ref),
            (own_hbm, inner_ref),
        ],
        sems,
    )
    for copy in copies[:4]:
        copy.wait()
    sub = row % UPS
    spread = (dot(from_peer_ref[...], recv_ref[:, 0, :]) * in_lanes_ref[...].astype(F32)).astype(BF16)
    u_before = dot(spread, taps_ref[:, :CH]).astype(BF16)
    before = silu(u_before.astype(F32)).astype(BF16)
    u_ref[...] = dot(spread, taps_ref[:, CH:]).astype(BF16)
    now = silu(u_ref[...].astype(F32)).astype(BF16)
    v_ref[:, :CH] = jnp.where(sub >= 2, now, before)
    v_ref[:, CH : 2 * CH] = jnp.where(sub >= 1, now, before)
    v_ref[:, 2 * CH :] = now
    copies[4].wait()
    total = u_ref[...].astype(F32) + dot(v_ref[...], w_time_ref[...].reshape(3 * CH, CH))
    x_ref[...] = total.astype(BF16)
    x_own_ref[...] = x_ref[:, pl.ds(pl.multiple_of(section * 128, 128), 128)]
    norm_silu(x_ref, h_ref, CH)
    copies[5].wait()
    inner_quarters(h_ref, [inner_ref], acc_ref, h1_ref, h2_ref)


def cross_kernel(h_hbm, cross_hbm, cross_swap_hbm, h2_ref, h_ref, inner_ref, acc_ref, h1_ref, sems):
    row, _ = my_place()
    mine, other = halves(row % 2)
    pairs = [
        (h_hbm, h_ref),
        (cross_hbm, inner_ref.at[:, :, mine, :]),
        (cross_swap_hbm, inner_ref.at[:, :, other, :]),
    ]
    for copy in start_all(pairs, sems):
        copy.wait()
    inner_quarters(h_ref, [inner_ref], acc_ref, h1_ref, h2_ref)


def slots(w_hbm, outer_ref, which):
    section = lax.axis_index("section").astype(jnp.int32)
    pairs = []
    for n, slot in enumerate(which):
        lanes = pl.ds(pl.multiple_of((section ^ slot) * 128, 128), 128)
        pairs.append((w_hbm.at[:, :, lanes, :], outer_ref.at[:, :, n * 128 : (n + 1) * 128, :]))
    return pairs


def second_kernel(x_own_hbm, own_hbm, pair_hbm, cross_hbm, w_hbm, out_ref, x_own_ref, all_ref, outer_ref, acc_ref, sems):
    pairs = slots(w_hbm, outer_ref, (0, 1, 3))
    for n, h2_hbm in enumerate((own_hbm, pair_hbm, cross_hbm)):
        pairs.append((h2_hbm, all_ref.at[:, n * 128 : (n + 1) * 128]))
    for copy in start_all(pairs + [(x_own_hbm, x_own_ref)], sems):
        copy.wait()
    conv(all_ref, [outer_ref], acc_ref)
    for i in range(HS):
        rows = slice(i * W, (i + 1) * W)
        out_ref[rows, :] = x_own_ref[rows, :].astype(F32) + gathered(acc_ref, i)


def third_kernel(part_hbm, far_hbm, w_hbm, out_ref, outer_ref, acc_ref, far_ref, part_ref, sems):
    copies = start_all(slots(w_hbm, outer_ref, (2,)) + [(far_hbm, far_ref), (part_hbm, part_ref)], sems)
    for copy in copies[:2]:
        copy.wait()
    conv(far_ref, [outer_ref], acc_ref)
    copies[2].wait()
    for i in range(HS):
        out_ref[i] = (part_ref[i * W : (i + 1) * W, :] + gathered(acc_ref, i)).astype(BF16)


VM = pl.BlockSpec(memory_space=pltpu.VMEM)
HB = pl.BlockSpec(memory_space=pl.ANY)


def trade(value, across):
    pairs = []
    for row in range(FRAMES):
        for section in range(4):
            y = 4 * (row // 2 % 2) + section
            y = (((y + 1) ^ 1) - 1) % 8 if across else y ^ 1
            there = row // 4 * 4 + y // 4 * 2 + row % 2
            pairs.append((section * FRAMES + row, y % 4 * FRAMES + there))
    return lax.ppermute(value, ("section", "rows"), pairs)


def other_y_hi(value):
    pairs = []
    for row in range(FRAMES):
        for section in range(4):
            y = (4 * (row // 2 % 2) + section + (2 if section >= 2 else -2)) % 8
            there = row // 4 * 4 + y // 4 * 2 + row % 2
            pairs.append((section * FRAMES + row, y % 4 * FRAMES + there))
    return lax.ppermute(value, ("section", "rows"), pairs)


def swap(value):
    return lax.ppermute(value, "rows", [(row, row ^ 1) for row in range(FRAMES)])


def block(latents, w_in, w_time, w_first, w_second):
    pack_constants, cell_constants = layouts()
    lat = latents.transpose(0, 3, 2, 1).reshape(CLIPS * LOCAL, LATC, LF)
    lat_other = other_y_hi(lat)
    core = lax.axis_index("rows").astype(jnp.int32) % 2
    half = lax.dynamic_slice_in_dim(w_first, core * 256, 256, 2)
    cross = trade(half, True)
    packed = pl.pallas_call(
        pack_kernel,
        out_shape=jax.ShapeDtypeStruct((PEERS, 1, MSG), BF16),
        in_specs=[VM] * 5,
        out_specs=VM,
        scratch_shapes=[pltpu.VMEM((MSG, LF), F32)],
    )(lat, lat_other, *pack_constants)
    groups = [[row for row in range(FRAMES) if row // 2 % 2 == y_hi] for y_hi in range(2)]
    recv = lax.all_to_all(packed, "rows", split_axis=0, concat_axis=0, axis_index_groups=groups, tiled=True)
    cross_swap = swap(cross)
    taps = pl.pallas_call(
        taps_kernel,
        out_shape=jax.ShapeDtypeStruct((MSG, 2 * CH), BF16),
        in_specs=[VM],
        out_specs=VM,
        scratch_shapes=[pltpu.VMEM((16, CH), F32)],
        compiler_params=pltpu.CompilerParams(vmem_limit_bytes=67_000_000),
    )(w_in)
    x_own, h, h2_own = pl.pallas_call(
        first_kernel,
        out_shape=[
            jax.ShapeDtypeStruct((CELLS, 128), BF16),
            jax.ShapeDtypeStruct((CELLS, CH), BF16),
            jax.ShapeDtypeStruct((CELLS, 128), BF16),
        ],
        in_specs=[HB] * 6,
        out_specs=[VM] * 3,
        scratch_shapes=[
            pltpu.VMEM((PEERS, 1, MSG), BF16),
            pltpu.VMEM((CELLS, PEERS), BF16),
            pltpu.VMEM((CELLS, MSG), BF16),
            pltpu.VMEM((MSG, 2 * CH), BF16),
            pltpu.VMEM((3, CH, CH), BF16),
            pltpu.VMEM((3, 3, CH, 128), BF16),
            pltpu.VMEM((CELLS, CH), BF16),
            pltpu.VMEM((CELLS, 3 * CH), BF16),
            pltpu.VMEM((CELLS, CH), BF16),
            pltpu.VMEM((CELLS, 384), F32),
            pltpu.VMEM((CELLS, 128), BF16),
            pltpu.SemaphoreType.DMA((6,)),
        ],
    )(recv, *cell_constants, taps, w_time, w_first)
    h2_pair = trade(h2_own, False)
    h2_cross = pl.pallas_call(
        cross_kernel,
        out_shape=jax.ShapeDtypeStruct((CELLS, 128), BF16),
        in_specs=[HB] * 3,
        out_specs=VM,
        scratch_shapes=[
            pltpu.VMEM((CELLS, CH), BF16),
            pltpu.VMEM((3, 3, CH, 128), BF16),
            pltpu.VMEM((CELLS, 384), F32),
            pltpu.VMEM((CELLS, 128), BF16),
            pltpu.SemaphoreType.DMA((3,)),
        ],
        compiler_params=pltpu.CompilerParams(vmem_limit_bytes=67_000_000),
    )(h, cross, cross_swap)
    far = trade(h2_cross, False)
    part = pl.pallas_call(
        second_kernel,
        out_shape=jax.ShapeDtypeStruct((CELLS, 128), F32),
        in_specs=[HB] * 5,
        out_specs=VM,
        scratch_shapes=[
            pltpu.VMEM((CELLS, 128), BF16),
            pltpu.VMEM((CELLS, 384), BF16),
            pltpu.VMEM((3, 3, 384, 128), BF16),
            pltpu.VMEM((CELLS, 384), F32),
            pltpu.SemaphoreType.DMA((7,)),
        ],
        compiler_params=pltpu.CompilerParams(vmem_limit_bytes=67_000_000),
    )(x_own, h2_own, h2_pair, h2_cross, w_second)
    out = pl.pallas_call(
        third_kernel,
        out_shape=jax.ShapeDtypeStruct((HS, W, 128), BF16),
        in_specs=[HB] * 3,
        out_specs=VM,
        scratch_shapes=[
            pltpu.VMEM((3, 3, 128, 128), BF16),
            pltpu.VMEM((CELLS, 384), F32),
            pltpu.VMEM((CELLS, 128), BF16),
            pltpu.VMEM((CELLS, 128), F32),
            pltpu.SemaphoreType.DMA((3,)),
        ],
    )(part, far, w_second)
    return out.reshape(1, HS, W, 128)


def solution(mesh):
    in_specs = (
        P(None, None, None, "rows"),
        P(),
        P(),
        P(None, None, None, "section"),
        P(None, None, None, "section"),
    )
    out_specs = P("rows", None, None, "section")
    return jax.shard_map(block, mesh=mesh, in_specs=in_specs, out_specs=out_specs, check_vma=False)
```

```python
import jax
import jax.numpy as jnp
import numpy as np
from jax import lax
from jax.experimental import pallas as pl
from jax.experimental.pallas import tpu as pltpu
from jax.sharding import PartitionSpec as P


CH = 512
LATC = 4
HS = 4
W = 160
CELLS = HS * W
CLIPS = 4
LF = 8
UPS = 4
FRAMES = 128
GROUP = 16
LOCAL = 5
WINDOW = 4
MSG = 2 * LOCAL * WINDOW * LATC
PEERS = 64
STEP = 128

F32 = jnp.float32
BF16 = jnp.bfloat16


def dot(a, b):
    return jnp.dot(a, b, preferred_element_type=F32)


def iota(shape, dim):
    return lax.broadcasted_iota(jnp.int32, shape, dim)


def onehot(cond):
    return jnp.where(cond, 1.0, 0.0).astype(BF16)


def silu(t):
    return 0.5 * t * (1.0 + jnp.tanh(0.5 * t))


def layouts():
    peer = np.arange(PEERS)[:, None]
    row = np.arange(MSG)
    lane = np.arange(MSG)
    picks = [np.arange(LF)[None] == np.maximum(peer % 16 // 2 - 3 + j, 0) for j in range(WINDOW)]
    same_clip = peer // 16 == row[None] // 20 % CLIPS
    home = (row // 80 * LOCAL + row // LATC % LOCAL)[:, None] == lane[None] // 16
    home = home & (row[:, None] % LATC == lane[None] % LATC)
    places = [home & (lane[None] // LATC % WINDOW == j) for j in range(WINDOW)]
    cell = np.arange(CELLS)[:, None]
    owner = cell // LOCAL
    from_peer = np.arange(PEERS)[None] == owner // 4 * 2 + owner % 2
    in_lanes = lane[None] // 16 == owner // 2 % 2 * LOCAL + cell % LOCAL
    pack = jnp.asarray(np.stack(picks), BF16), jnp.asarray(same_clip, F32), jnp.asarray(np.stack(places), BF16)
    return pack, (jnp.asarray(from_peer, BF16), jnp.asarray(in_lanes, BF16))


def pack_kernel(lat_ref, other_ref, pick_ref, same_clip_ref, place_ref, out_ref, flat_ref):
    upper = lax.axis_index("rows") // 2 % 2 == 1
    for n in range(CLIPS * LOCAL):
        mine = lat_ref[n].astype(F32)
        theirs = other_ref[n].astype(F32)
        flat_ref[n * LATC : (n + 1) * LATC, :] = jnp.where(upper, theirs, mine)
        flat_ref[80 + n * LATC : 80 + (n + 1) * LATC, :] = jnp.where(upper, mine, theirs)
    flat = flat_ref[...].astype(BF16)
    total = jnp.zeros((PEERS, MSG), F32)
    for j in range(WINDOW):
        taken = lax.dot_general(pick_ref[j], flat, (((1,), (1,)), ((), ())), preferred_element_type=F32)
        total = total + dot((taken * same_clip_ref[...]).astype(BF16), place_ref[j])
    out_ref[:, 0, :] = total.astype(BF16)


def group_total(sums):
    lane = iota(sums.shape, 1)
    width = sums.shape[1]
    for d in (1, 2, 4, 8):
        up = pltpu.roll(sums, d, 1)
        down = pltpu.roll(sums, width - d, 1)
        sums = sums + jnp.where((lane & d) != 0, up, down)
    return sums


def norm_silu(src_ref, dst_ref, width):
    count = float(CELLS * GROUP)

    def tree(t):
        t = t.reshape(-1, 8, width)
        while t.shape[0] > 1:
            t = t[: t.shape[0] // 2] + t[t.shape[0] // 2 :]
        return t[0]

    def total(part):
        part = jnp.sum(part, axis=0, keepdims=True)
        return group_total(jnp.broadcast_to(part, (8, width)))[:1] / count

    part = jnp.zeros((8, width), F32)
    for r in range(0, CELLS, STEP):
        part = part + tree(src_ref[r : r + STEP, :].astype(F32))
    mean = total(part)
    part = jnp.zeros((8, width), F32)
    for r in range(0, CELLS, STEP):
        t = src_ref[r : r + STEP, :].astype(F32) - mean
        part = part + tree(t * t)
    scale = lax.rsqrt(total(part) + 1e-06)
    for r in range(0, CELLS, STEP):
        t = (src_ref[r : r + STEP, :].astype(F32) - mean) * scale
        dst_ref[r : r + STEP, :] = silu(t).astype(BF16)


def conv(h_ref, weights, acc_ref):
    for dy in (1, 0, 2):
        src = slice(W, CELLS) if dy == 2 else slice(0, CELLS - W) if dy == 0 else slice(0, CELLS)
        dst = slice(W, CELLS) if dy == 0 else slice(0, CELLS - W) if dy == 2 else slice(0, CELLS)
        w = jnp.concatenate([ref[dy, dx] for ref in weights for dx in range(3)], axis=1)
        if dy == 1:
            acc_ref[...] = dot(h_ref[src, :], w)
        else:
            acc_ref[dst, :] += dot(h_ref[src, :], w)


def gathered(acc_ref, i, base=0):
    rows = slice(i * W, (i + 1) * W)
    col = iota((W, 128), 0)
    left = jnp.where(col == 0, 0.0, pltpu.roll(acc_ref[rows, base : base + 128], 1, 0))
    right = jnp.where(col == W - 1, 0.0, pltpu.roll(acc_ref[rows, base + 256 : base + 384], W - 1, 0))
    return left + acc_ref[rows, base + 128 : base + 256] + right


def halves(core):
    mine = pl.ds(pl.multiple_of(core * 256, 256), 256)
    other = pl.ds(pl.multiple_of(256 - core * 256, 256), 256)
    return mine, other


def start_all(pairs, sems):
    copies = [pltpu.make_async_copy(src, dst, sems.at[n]) for n, (src, dst) in enumerate(pairs)]
    for copy in copies:
        copy.start()
    return copies


def my_place():
    return lax.axis_index("rows").astype(jnp.int32), lax.axis_index("section").astype(jnp.int32)


def inner_quarters(h_ref, weights, acc_ref, h1_ref, dst_ref):
    conv(h_ref, weights, acc_ref)
    for n in range(len(weights)):
        for i in range(HS):
            h1_ref[i * W : (i + 1) * W, n * 128 : (n + 1) * 128] = gathered(acc_ref, i, n * 384).astype(BF16)
    norm_silu(h1_ref, dst_ref, len(weights) * 128)


def taps_kernel(w_in_ref, out_ref, taps_ref):
    taps_ref[...] = jnp.zeros_like(taps_ref)
    for k in range(3):
        taps_ref[k * LATC : (k + 1) * LATC, :] = w_in_ref[k].astype(F32)
    taps = taps_ref[...].astype(BF16)
    lane = iota((MSG, 16), 0) % 16
    tap = iota((MSG, 16), 1)
    for s in range(2):
        out_ref[:, s * CH : (s + 1) * CH] = dot(onehot(lane == tap + s * LATC), taps).astype(BF16)


def first_kernel(recv_hbm, from_peer_hbm, in_lanes_hbm, taps_hbm, w_time_hbm, own_hbm, x_own_ref, h_ref, h2_ref,
                 recv_ref, from_peer_ref, in_lanes_ref, taps_ref, w_time_ref, inner_ref, u_ref, v_ref, x_ref,
                 acc_ref, h1_ref, sems):
    row, section = my_place()
    copies = start_all(
        [
            (recv_hbm, recv_ref),
            (from_peer_hbm, from_peer_ref),
            (in_lanes_hbm, in_lanes_ref),
            (taps_hbm, taps_ref),
            (w_time_hbm, w_time_ref),
            (own_hbm, inner_ref),
        ],
        sems,
    )
    for copy in copies[:4]:
        copy.wait()
    sub = row % UPS
    spread = (dot(from_peer_ref[...], recv_ref[:, 0, :]) * in_lanes_ref[...].astype(F32)).astype(BF16)
    u_before = dot(spread, taps_ref[:, :CH]).astype(BF16)
    before = silu(u_before.astype(F32)).astype(BF16)
    u_ref[...] = dot(spread, taps_ref[:, CH:]).astype(BF16)
    now = silu(u_ref[...].astype(F32)).astype(BF16)
    v_ref[:, :CH] = jnp.where(sub >= 2, now, before)
    v_ref[:, CH : 2 * CH] = jnp.where(sub >= 1, now, before)
    v_ref[:, 2 * CH :] = now
    copies[4].wait()
    total = u_ref[...].astype(F32) + dot(v_ref[...], w_time_ref[...].reshape(3 * CH, CH))
    x_ref[...] = total.astype(BF16)
    x_own_ref[...] = x_ref[:, pl.ds(pl.multiple_of(section * 128, 128), 128)]
    norm_silu(x_ref, h_ref, CH)
    copies[5].wait()
    inner_quarters(h_ref, [inner_ref], acc_ref, h1_ref, h2_ref)


def cross_kernel(h_hbm, cross_hbm, cross_swap_hbm, h2_ref, h_ref, inner_ref, acc_ref, h1_ref, sems):
    row, _ = my_place()
    mine, other = halves(row % 2)
    pairs = [
        (h_hbm, h_ref),
        (cross_hbm, inner_ref.at[:, :, mine, :]),
        (cross_swap_hbm, inner_ref.at[:, :, other, :]),
    ]
    for copy in start_all(pairs, sems):
        copy.wait()
    inner_quarters(h_ref, [inner_ref], acc_ref, h1_ref, h2_ref)


def slots(w_hbm, outer_ref, which):
    section = lax.axis_index("section").astype(jnp.int32)
    pairs = []
    for n, slot in enumerate(which):
        lanes = pl.ds(pl.multiple_of((section ^ slot) * 128, 128), 128)
        pairs.append((w_hbm.at[:, :, lanes, :], outer_ref.at[:, :, n * 128 : (n + 1) * 128, :]))
    return pairs


def second_kernel(x_own_hbm, own_hbm, pair_hbm, cross_hbm, w_hbm, out_ref, x_own_ref, all_ref, outer_ref, acc_ref, sems):
    pairs = slots(w_hbm, outer_ref, (0, 1, 3))
    for n, h2_hbm in enumerate((own_hbm, pair_hbm, cross_hbm)):
        pairs.append((h2_hbm, all_ref.at[:, n * 128 : (n + 1) * 128]))
    for copy in start_all(pairs + [(x_own_hbm, x_own_ref)], sems):
        copy.wait()
    conv(all_ref, [outer_ref], acc_ref)
    for i in range(HS):
        rows = slice(i * W, (i + 1) * W)
        out_ref[rows, :] = x_own_ref[rows, :].astype(F32) + gathered(acc_ref, i)


def third_kernel(part_hbm, far_hbm, w_hbm, out_ref, outer_ref, acc_ref, far_ref, part_ref, sems):
    copies = start_all(slots(w_hbm, outer_ref, (2,)) + [(far_hbm, far_ref), (part_hbm, part_ref)], sems)
    for copy in copies[:2]:
        copy.wait()
    conv(far_ref, [outer_ref], acc_ref)
    copies[2].wait()
    for i in range(HS):
        out_ref[i] = (part_ref[i * W : (i + 1) * W, :] + gathered(acc_ref, i)).astype(BF16)


VM = pl.BlockSpec(memory_space=pltpu.VMEM)
HB = pl.BlockSpec(memory_space=pl.ANY)


def trade(value, across):
    pairs = []
    for row in range(FRAMES):
        for section in range(4):
            y = 4 * (row // 2 % 2) + section
            y = (((y + 1) ^ 1) - 1) % 8 if across else y ^ 1
            there = row // 4 * 4 + y // 4 * 2 + row % 2
            pairs.append((section * FRAMES + row, y % 4 * FRAMES + there))
    return lax.ppermute(value, ("section", "rows"), pairs)


def other_y_hi(value):
    pairs = []
    for row in range(FRAMES):
        for section in range(4):
            y = (4 * (row // 2 % 2) + section + (2 if section >= 2 else -2)) % 8
            there = row // 4 * 4 + y // 4 * 2 + row % 2
            pairs.append((section * FRAMES + row, y % 4 * FRAMES + there))
    return lax.ppermute(value, ("section", "rows"), pairs)


def swap(value):
    return lax.ppermute(value, "rows", [(row, row ^ 1) for row in range(FRAMES)])


def block(latents, w_in, w_time, w_first, w_second):
    pack_constants, cell_constants = layouts()
    lat = latents.transpose(0, 3, 2, 1).reshape(CLIPS * LOCAL, LATC, LF)
    lat_other = other_y_hi(lat)
    core = lax.axis_index("rows").astype(jnp.int32) % 2
    half = lax.dynamic_slice_in_dim(w_first, core * 256, 256, 2)
    cross = trade(half, True)
    packed = pl.pallas_call(
        pack_kernel,
        out_shape=jax.ShapeDtypeStruct((PEERS, 1, MSG), BF16),
        in_specs=[VM] * 5,
        out_specs=VM,
        scratch_shapes=[pltpu.VMEM((MSG, LF), F32)],
    )(lat, lat_other, *pack_constants)
    groups = [[row for row in range(FRAMES) if row // 2 % 2 == y_hi] for y_hi in range(2)]
    recv = lax.all_to_all(packed, "rows", split_axis=0, concat_axis=0, axis_index_groups=groups, tiled=True)
    cross_swap = swap(cross)
    taps = pl.pallas_call(
        taps_kernel,
        out_shape=jax.ShapeDtypeStruct((MSG, 2 * CH), BF16),
        in_specs=[VM],
        out_specs=VM,
        scratch_shapes=[pltpu.VMEM((16, CH), F32)],
        compiler_params=pltpu.CompilerParams(vmem_limit_bytes=67_000_000),
    )(w_in)
    first = pl.pallas_call(
        first_kernel,
        out_shape=[
            jax.ShapeDtypeStruct((CELLS, 128), BF16),
            jax.ShapeDtypeStruct((CELLS, CH), BF16),
            jax.ShapeDtypeStruct((CELLS, 128), BF16),
        ],
        in_specs=[HB] * 6,
        compiler_params=pltpu.CompilerParams(vmem_limit_bytes=67_000_000),
        out_specs=[VM] * 3,
        scratch_shapes=[
            pltpu.VMEM((PEERS, 1, MSG), BF16),
            pltpu.VMEM((CELLS, PEERS), BF16),
            pltpu.VMEM((CELLS, MSG), BF16),
            pltpu.VMEM((MSG, 2 * CH), BF16),
            pltpu.VMEM((3, CH, CH), BF16),
            pltpu.VMEM((3, 3, CH, 128), BF16),
            pltpu.VMEM((CELLS, CH), BF16),
            pltpu.VMEM((CELLS, 3 * CH), BF16),
            pltpu.VMEM((CELLS, CH), BF16),
            pltpu.VMEM((CELLS, 384), F32),
            pltpu.VMEM((CELLS, 128), BF16),
            pltpu.SemaphoreType.DMA((6,)),
        ],
    )
    x_own, h, h2_own = first(recv, *cell_constants, taps, w_time, w_first)
    h2_pair = trade(h2_own, False)
    h2_cross = pl.pallas_call(
        cross_kernel,
        out_shape=jax.ShapeDtypeStruct((CELLS, 128), BF16),
        in_specs=[HB] * 3,
        out_specs=VM,
        scratch_shapes=[
            pltpu.VMEM((CELLS, CH), BF16),
            pltpu.VMEM((3, 3, CH, 128), BF16),
            pltpu.VMEM((CELLS, 384), F32),
            pltpu.VMEM((CELLS, 128), BF16),
            pltpu.SemaphoreType.DMA((3,)),
        ],
        compiler_params=pltpu.CompilerParams(vmem_limit_bytes=67_000_000),
    )(h, cross, cross_swap)
    far = trade(h2_cross, False)
    part = pl.pallas_call(
        second_kernel,
        out_shape=jax.ShapeDtypeStruct((CELLS, 128), F32),
        in_specs=[HB] * 5,
        out_specs=VM,
        scratch_shapes=[
            pltpu.VMEM((CELLS, 128), BF16),
            pltpu.VMEM((CELLS, 384), BF16),
            pltpu.VMEM((3, 3, 384, 128), BF16),
            pltpu.VMEM((CELLS, 384), F32),
            pltpu.SemaphoreType.DMA((7,)),
        ],
        compiler_params=pltpu.CompilerParams(vmem_limit_bytes=67_000_000),
    )(x_own, h2_own, h2_pair, h2_cross, w_second)
    out = pl.pallas_call(
        third_kernel,
        out_shape=jax.ShapeDtypeStruct((HS, W, 128), BF16),
        in_specs=[HB] * 3,
        out_specs=VM,
        scratch_shapes=[
            pltpu.VMEM((3, 3, 128, 128), BF16),
            pltpu.VMEM((CELLS, 384), F32),
            pltpu.VMEM((CELLS, 128), BF16),
            pltpu.VMEM((CELLS, 128), F32),
            pltpu.SemaphoreType.DMA((3,)),
        ],
    )(part, far, w_second)
    return out.reshape(1, HS, W, 128)


def solution(mesh):
    in_specs = (
        P(None, None, None, "rows"),
        P(),
        P(),
        P(None, None, None, "section"),
        P(None, None, None, "section"),
    )
    out_specs = P("rows", None, None, "section")
    return jax.shard_map(block, mesh=mesh, in_specs=in_specs, out_specs=out_specs, check_vma=False)
```

```python
import jax
import jax.numpy as jnp
import numpy as np
from jax import lax
from jax.experimental import pallas as pl
from jax.experimental.pallas import tpu as pltpu
from jax.sharding import PartitionSpec as P


CH = 512
LATC = 4
HS = 4
W = 160
CELLS = HS * W
CLIPS = 4
LF = 8
UPS = 4
FRAMES = 128
GROUP = 16
LOCAL = 5
WINDOW = 4
MSG = 2 * LOCAL * WINDOW * LATC
PEERS = 64
STEP = 128

F32 = jnp.float32
BF16 = jnp.bfloat16


def dot(a, b):
    return jnp.dot(a, b, preferred_element_type=F32)


def iota(shape, dim):
    return lax.broadcasted_iota(jnp.int32, shape, dim)


def onehot(cond):
    return jnp.where(cond, 1.0, 0.0).astype(BF16)


def silu(t):
    return 0.5 * t * (1.0 + jnp.tanh(0.5 * t))


def layouts():
    peer = np.arange(PEERS)[:, None]
    row = np.arange(MSG)
    lane = np.arange(MSG)
    picks = [np.arange(LF)[None] == np.maximum(peer % 16 // 2 - 3 + j, 0) for j in range(WINDOW)]
    same_clip = peer // 16 == row[None] // 20 % CLIPS
    home = (row // 80 * LOCAL + row // LATC % LOCAL)[:, None] == lane[None] // 16
    home = home & (row[:, None] % LATC == lane[None] % LATC)
    cell = np.arange(CELLS)[:, None]
    owner = cell // LOCAL
    from_peer = np.arange(PEERS)[None] == owner // 4 * 2 + owner % 2
    in_lanes = lane[None] // 16 == owner // 2 % 2 * LOCAL + cell % LOCAL
    pack = jnp.asarray(np.stack(picks), BF16), jnp.asarray(same_clip, F32), jnp.asarray(home, BF16)
    return pack, (jnp.asarray(from_peer, BF16), jnp.asarray(in_lanes, BF16))


def pack_kernel(lat_ref, other_ref, pick_ref, same_clip_ref, place_ref, out_ref, flat_ref):
    upper = lax.axis_index("rows") // 2 % 2 == 1
    for n in range(CLIPS * LOCAL):
        mine = lat_ref[n].astype(F32)
        theirs = other_ref[n].astype(F32)
        flat_ref[n * LATC : (n + 1) * LATC, :] = jnp.where(upper, theirs, mine)
        flat_ref[80 + n * LATC : 80 + (n + 1) * LATC, :] = jnp.where(upper, mine, theirs)
    flat = flat_ref[...].astype(BF16)
    entry = iota((PEERS, MSG), 1) // LATC % WINDOW
    for j in range(WINDOW):
        taken = lax.dot_general(pick_ref[j], flat, (((1,), (1,)), ((), ())), preferred_element_type=F32)
        placed = dot((taken * same_clip_ref[...]).astype(BF16), place_ref[...])
        total = placed if j == 0 else jnp.where(entry == j, placed, total)
    out_ref[:, 0, :] = total.astype(BF16)


def group_total(sums):
    lane = iota(sums.shape, 1)
    width = sums.shape[1]
    for d in (1, 2, 4, 8):
        up = pltpu.roll(sums, d, 1)
        down = pltpu.roll(sums, width - d, 1)
        sums = sums + jnp.where((lane & d) != 0, up, down)
    return sums


def norm_silu(src_ref, dst_ref, width):
    count = float(CELLS * GROUP)

    def tree(t):
        t = t.reshape(-1, 8, width)
        while t.shape[0] > 1:
            t = t[: t.shape[0] // 2] + t[t.shape[0] // 2 :]
        return t[0]

    def total(part):
        part = jnp.sum(part, axis=0, keepdims=True)
        return group_total(jnp.broadcast_to(part, (8, width)))[:1] / count

    part = jnp.zeros((8, width), F32)
    for r in range(0, CELLS, STEP):
        part = part + tree(src_ref[r : r + STEP, :].astype(F32))
    mean = total(part)
    part = jnp.zeros((8, width), F32)
    for r in range(0, CELLS, STEP):
        t = src_ref[r : r + STEP, :].astype(F32) - mean
        part = part + tree(t * t)
    scale = lax.rsqrt(total(part) + 1e-06)
    for r in range(0, CELLS, STEP):
        t = (src_ref[r : r + STEP, :].astype(F32) - mean) * scale
        dst_ref[r : r + STEP, :] = silu(t).astype(BF16)


def conv(h_ref, weights, acc_ref):
    for dy in (1, 0, 2):
        src = slice(W, CELLS) if dy == 2 else slice(0, CELLS - W) if dy == 0 else slice(0, CELLS)
        dst = slice(W, CELLS) if dy == 0 else slice(0, CELLS - W) if dy == 2 else slice(0, CELLS)
        w = jnp.concatenate([ref[dy, dx] for ref in weights for dx in range(3)], axis=1)
        if dy == 1:
            acc_ref[...] = dot(h_ref[src, :], w)
        else:
            acc_ref[dst, :] += dot(h_ref[src, :], w)


def gathered(acc_ref, i, base=0):
    rows = slice(i * W, (i + 1) * W)
    col = iota((W, 128), 0)
    left = jnp.where(col == 0, 0.0, pltpu.roll(acc_ref[rows, base : base + 128], 1, 0))
    right = jnp.where(col == W - 1, 0.0, pltpu.roll(acc_ref[rows, base + 256 : base + 384], W - 1, 0))
    return left + acc_ref[rows, base + 128 : base + 256] + right


def halves(core):
    mine = pl.ds(pl.multiple_of(core * 256, 256), 256)
    other = pl.ds(pl.multiple_of(256 - core * 256, 256), 256)
    return mine, other


def start_all(pairs, sems):
    copies = [pltpu.make_async_copy(src, dst, sems.at[n]) for n, (src, dst) in enumerate(pairs)]
    for copy in copies:
        copy.start()
    return copies


def my_place():
    return lax.axis_index("rows").astype(jnp.int32), lax.axis_index("section").astype(jnp.int32)


def inner_quarters(h_ref, weights, acc_ref, h1_ref, dst_ref):
    conv(h_ref, weights, acc_ref)
    for n in range(len(weights)):
        for i in range(HS):
            h1_ref[i * W : (i + 1) * W, n * 128 : (n + 1) * 128] = gathered(acc_ref, i, n * 384).astype(BF16)
    norm_silu(h1_ref, dst_ref, len(weights) * 128)


def taps_kernel(w_in_ref, out_ref, taps_ref):
    taps_ref[...] = jnp.zeros_like(taps_ref)
    for k in range(3):
        taps_ref[k * LATC : (k + 1) * LATC, :] = w_in_ref[k].astype(F32)
    taps = taps_ref[...].astype(BF16)
    lane = iota((MSG, 16), 0) % 16
    tap = iota((MSG, 16), 1)
    for s in range(2):
        out_ref[:, s * CH : (s + 1) * CH] = dot(onehot(lane == tap + s * LATC), taps).astype(BF16)


def first_kernel(recv_hbm, from_peer_hbm, in_lanes_hbm, taps_hbm, w_time_hbm, own_hbm, cross_hbm, cross_swap_hbm,
                 x_own_ref, h2_ref,
                 recv_ref, from_peer_ref, in_lanes_ref, taps_ref, w_time_ref, inner_ref, u_ref, v_ref, x_ref, h_ref,
                 acc_ref, h1_ref, sems):
    row, section = my_place()
    mine, other = halves(row % 2)
    copies = start_all(
        [
            (recv_hbm, recv_ref),
            (from_peer_hbm, from_peer_ref),
            (in_lanes_hbm, in_lanes_ref),
            (taps_hbm, taps_ref),
            (w_time_hbm, w_time_ref),
            (own_hbm, inner_ref.at[0]),
            (cross_hbm, inner_ref.at[1, :, :, mine, :]),
            (cross_swap_hbm, inner_ref.at[1, :, :, other, :]),
        ],
        sems,
    )
    for copy in copies[:4]:
        copy.wait()
    sub = row % UPS
    spread = (dot(from_peer_ref[...], recv_ref[:, 0, :]) * in_lanes_ref[...].astype(F32)).astype(BF16)
    u_before = dot(spread, taps_ref[:, :CH]).astype(BF16)
    before = silu(u_before.astype(F32)).astype(BF16)
    u_ref[...] = dot(spread, taps_ref[:, CH:]).astype(BF16)
    now = silu(u_ref[...].astype(F32)).astype(BF16)
    v_ref[:, :CH] = jnp.where(sub >= 2, now, before)
    v_ref[:, CH : 2 * CH] = jnp.where(sub >= 1, now, before)
    v_ref[:, 2 * CH :] = now
    copies[4].wait()
    total = u_ref[...].astype(F32) + dot(v_ref[...], w_time_ref[...].reshape(3 * CH, CH))
    x_ref[...] = total.astype(BF16)
    x_own_ref[...] = x_ref[:, pl.ds(pl.multiple_of(section * 128, 128), 128)]
    norm_silu(x_ref, h_ref, CH)
    for copy in copies[5:]:
        copy.wait()
    inner_quarters(h_ref, [inner_ref.at[0], inner_ref.at[1]], acc_ref, h1_ref, h2_ref)


def two_slots(w_hbm, outer_ref, slots):
    section = lax.axis_index("section").astype(jnp.int32)
    pairs = []
    for n, slot in enumerate(slots):
        lanes = pl.ds(pl.multiple_of((section ^ slot) * 128, 128), 128)
        pairs.append((w_hbm.at[:, :, lanes, :], outer_ref.at[:, :, n * 128 : (n + 1) * 128, :]))
    return pairs


def second_kernel(x_own_ref, h2_ref, w_hbm, out_ref, outer_ref, acc_ref, sems):
    for copy in start_all(two_slots(w_hbm, outer_ref, (0, 3)), sems):
        copy.wait()
    conv(h2_ref, [outer_ref], acc_ref)
    for i in range(HS):
        rows = slice(i * W, (i + 1) * W)
        out_ref[rows, :] = x_own_ref[rows, :].astype(F32) + gathered(acc_ref, i)


def third_kernel(part_hbm, far_hbm, w_hbm, out_ref, outer_ref, acc_ref, far_ref, part_ref, sems):
    copies = start_all(two_slots(w_hbm, outer_ref, (1, 2)) + [(far_hbm, far_ref), (part_hbm, part_ref)], sems)
    for copy in copies[:3]:
        copy.wait()
    conv(far_ref, [outer_ref], acc_ref)
    copies[3].wait()
    for i in range(HS):
        out_ref[i] = (part_ref[i * W : (i + 1) * W, :] + gathered(acc_ref, i)).astype(BF16)


VM = pl.BlockSpec(memory_space=pltpu.VMEM)
HB = pl.BlockSpec(memory_space=pl.ANY)


def trade(value, across):
    pairs = []
    for row in range(FRAMES):
        for section in range(4):
            y = 4 * (row // 2 % 2) + section
            y = (((y + 1) ^ 1) - 1) % 8 if across else y ^ 1
            there = row // 4 * 4 + y // 4 * 2 + row % 2
            pairs.append((section * FRAMES + row, y % 4 * FRAMES + there))
    return lax.ppermute(value, ("section", "rows"), pairs)


def other_y_hi(value):
    pairs = []
    for row in range(FRAMES):
        for section in range(4):
            y = (4 * (row // 2 % 2) + section + (2 if section >= 2 else -2)) % 8
            there = row // 4 * 4 + y // 4 * 2 + row % 2
            pairs.append((section * FRAMES + row, y % 4 * FRAMES + there))
    return lax.ppermute(value, ("section", "rows"), pairs)


def swap(value):
    return lax.ppermute(value, "rows", [(row, row ^ 1) for row in range(FRAMES)])


def block(latents, w_in, w_time, w_first, w_second):
    pack_constants, cell_constants = layouts()
    lat = latents.transpose(0, 3, 2, 1).reshape(CLIPS * LOCAL, LATC, LF)
    lat_other = other_y_hi(lat)
    core = lax.axis_index("rows").astype(jnp.int32) % 2
    half = lax.dynamic_slice_in_dim(w_first, core * 256, 256, 2)
    cross = trade(half, True)
    packed = pl.pallas_call(
        pack_kernel,
        out_shape=jax.ShapeDtypeStruct((PEERS, 1, MSG), BF16),
        in_specs=[VM] * 5,
        out_specs=VM,
        scratch_shapes=[pltpu.VMEM((MSG, LF), F32)],
    )(lat, lat_other, *pack_constants)
    groups = [[row for row in range(FRAMES) if row // 2 % 2 == y_hi] for y_hi in range(2)]
    recv = lax.all_to_all(packed, "rows", split_axis=0, concat_axis=0, axis_index_groups=groups, tiled=True)
    cross_swap = swap(cross)
    taps = pl.pallas_call(
        taps_kernel,
        out_shape=jax.ShapeDtypeStruct((MSG, 2 * CH), BF16),
        in_specs=[VM],
        out_specs=VM,
        scratch_shapes=[pltpu.VMEM((16, CH), F32)],
        compiler_params=pltpu.CompilerParams(vmem_limit_bytes=67_000_000),
    )(w_in)
    x_own, h2 = pl.pallas_call(
        first_kernel,
        out_shape=[
            jax.ShapeDtypeStruct((CELLS, 128), BF16),
            jax.ShapeDtypeStruct((CELLS, 256), BF16),
        ],
        in_specs=[HB] * 8,
        out_specs=[VM] * 2,
        scratch_shapes=[
            pltpu.VMEM((PEERS, 1, MSG), BF16),
            pltpu.VMEM((CELLS, PEERS), BF16),
            pltpu.VMEM((CELLS, MSG), BF16),
            pltpu.VMEM((MSG, 2 * CH), BF16),
            pltpu.VMEM((3, CH, CH), BF16),
            pltpu.VMEM((2, 3, 3, CH, 128), BF16),
            pltpu.VMEM((CELLS, CH), BF16),
            pltpu.VMEM((CELLS, 3 * CH), BF16),
            pltpu.VMEM((CELLS, CH), BF16),
            pltpu.VMEM((CELLS, CH), BF16),
            pltpu.VMEM((CELLS, 768), F32),
            pltpu.VMEM((CELLS, 256), BF16),
            pltpu.SemaphoreType.DMA((8,)),
        ],
    )(recv, *cell_constants, taps, w_time, w_first, cross, cross_swap)
    far = trade(h2, False)
    weights = [
        pltpu.VMEM((3, 3, 256, 128), BF16),
        pltpu.VMEM((CELLS, 384), F32),
        pltpu.SemaphoreType.DMA((2,)),
    ]
    part = pl.pallas_call(
        second_kernel,
        out_shape=jax.ShapeDtypeStruct((CELLS, 128), F32),
        in_specs=[VM, VM, HB],
        out_specs=VM,
        scratch_shapes=weights,
        compiler_params=pltpu.CompilerParams(vmem_limit_bytes=67_000_000),
    )(x_own, h2, w_second)
    out = pl.pallas_call(
        third_kernel,
        out_shape=jax.ShapeDtypeStruct((HS, W, 128), BF16),
        in_specs=[HB] * 3,
        out_specs=VM,
        scratch_shapes=weights[:2]
        + [
            pltpu.VMEM((CELLS, 256), BF16),
            pltpu.VMEM((CELLS, 128), F32),
            pltpu.SemaphoreType.DMA((4,)),
        ],
    )(part, far, w_second)
    return out.reshape(1, HS, W, 128)


def solution(mesh):
    in_specs = (
        P(None, None, None, "rows"),
        P(),
        P(),
        P(None, None, None, "section"),
        P(None, None, None, "section"),
    )
    out_specs = P("rows", None, None, "section")
    return jax.shard_map(block, mesh=mesh, in_specs=in_specs, out_specs=out_specs, check_vma=False)
```
